128 devices in a mesh: ctx: 16 (over z_lo, y, core), ch: 8 (over z_hi, x).
Axes of the slice: x: 4, y: 4, z: 4 (z_hi: 2, z_lo: 2; z = z_hi * 2 + z_lo), core: 2. Of those that a mesh axis runs over, the one named last changes fastest.
Arguments:
- q_vals: bfloat16 [8192, 4096], P('ch', 'ctx'), may hold values from -6 to 6
- k_vals: bfloat16 [8192, 4096], P('ch', 'ctx'), may hold values from -6 to 6
- v_vals: bfloat16 [8192, 4096], P('ch', 'ctx'), may hold values from -6 to 6
- grad_out: bfloat16 [8192, 4096], P('ch', 'ctx'), may hold values from -6 to 6
- exponents: int32 [3, 64, 32], P(None, 'ch', 'ctx'), may hold values from -2 to 1
- filter_taps: float32 [512, 1024], P('ch'), may hold values from -1 to 1
Outputs:
- grad_q: bfloat16 [8192, 4096], P('ch', 'ctx')
- grad_k: bfloat16 [8192, 4096], P('ch', 'ctx')
- grad_v: bfloat16 [8192, 4096], P('ch', 'ctx')
- grad_filter: float32 [512, 1024], P('ch', 'ctx')
- grad_amax: float32 [3, 32], P(None, 'ctx')
The draws below stay inside these ranges and needn't reach their ends.
All inputs are finite; a program needn't handle non-finite values.
Results may differ from the reference program's by a relative error of at most 0.0061.
Values may be sent and summed in bfloat16 or wider, within the bound.
No kernel may reach another device: no remote copies, remote signals or barrier semaphores. Data moves between devices by JAX's collectives and lax.ppermute only.
A program may use at most 128 MiB of HBM per device.

```python
import math
import jax
import jax.numpy as jnp
from jax import lax

D = 8192
FILTER_GROUPS = 512
QB = 128
SEQ = 4096
FILTER_TAP_COUNT = 1024


def draw_filter_taps(key, part):
    random_key_list = jax.random.split(jax.random.fold_in(key, 7), 7)
    slow_share = 0.5
    magnitude = jax.random.uniform(random_key_list[5], (FILTER_GROUPS, FILTER_TAP_COUNT), jnp.float32, 0.5, 1.5)
    slow = jax.random.bernoulli(random_key_list[0], slow_share, (FILTER_GROUPS, 1))
    fast_len = jax.random.uniform(random_key_list[1], (FILTER_GROUPS, 1), jnp.float32, 30.0, 50.0)
    slow_len = jnp.exp(jax.random.uniform(random_key_list[2], (FILTER_GROUPS, 1), jnp.float32, math.log(FILTER_TAP_COUNT * 1.0), math.log(FILTER_TAP_COUNT * 4.0)))
    length = jnp.where(slow, slow_len, fast_len)
    lag_location = jnp.arange(FILTER_TAP_COUNT, dtype=jnp.float32)[None, :]
    decay_profile = jnp.exp(-lag_location / length)
    spike_location = jax.random.randint(random_key_list[3], (FILTER_GROUPS, 2), 0, FILTER_TAP_COUNT).astype(jnp.float32)
    spike_retained = jax.random.uniform(random_key_list[4], (FILTER_GROUPS, 2), jnp.float32, 0.55, 0.8)
    for selected_variant in range(2):
        decay_profile = decay_profile * jnp.where(lag_location >= spike_location[:, selected_variant:selected_variant + 1], spike_retained[:, selected_variant:selected_variant + 1], 1.0)
    signs = jnp.where(jax.random.bernoulli(random_key_list[6], 0.5, (FILTER_GROUPS, FILTER_TAP_COUNT)), 1.0, -1.0)
    amplitude = jnp.sqrt(2.0 / length)
    return (amplitude * decay_profile * magnitude * signs).astype(jnp.float32)


def with_ends(entries, key, least, high):
    longest = entries.shape.index(max(entries.shape))
    spots = []
    for shift in (0, 1):
        where = [jax.random.randint(jax.random.fold_in(key, axis), (), 0, length) for axis, length in enumerate(entries.shape)]
        where[longest] = (where[longest] + shift) % entries.shape[longest]
        spots.append(tuple(where))
    return entries.at[spots[0]].set(least).at[spots[1]].set(high)


def level_of(stream_key, dims, cuts, smallest, top_value):
    gain = 1.0
    for dim, parts in cuts:
        steps = jax.random.uniform(jax.random.fold_in(jax.random.fold_in(stream_key, 6), dim), (parts,), jnp.float32, smallest / len(cuts), top_value / len(cuts))
        gain = gain * jnp.repeat(jnp.exp(steps), dims[dim] // parts).reshape((-1,) + (1,) * (len(dims) - 1 - dim))
    return gain


def gaussian(key, shape, width, reach, cuts=(), kind=jnp.bfloat16):
    loudness = level_of(key, shape, cuts, -0.22, 0.18) if cuts else 1.0
    values = jax.random.normal(key, shape, jnp.float32) * width * loudness
    return jnp.minimum(jnp.maximum(values, -reach), reach).astype(kind)


def setup_inputs(seed: int = 0) -> dict:
    key_of = jax.random.split(jax.random.key(seed), 7)
    q_vals = gaussian(key_of[0], (D, SEQ), 1.0, 6.0, ((0, 8), (1, 16)))
    k_vals = gaussian(key_of[1], (D, SEQ), 1.0, 6.0, ((0, 8), (1, 16)))
    v_vals = gaussian(key_of[2], (D, SEQ), 1.0, 6.0, ((0, 8), (1, 16)))
    grad_out = gaussian(key_of[3], (D, SEQ), 1.0, 6.0, ((0, 8), (1, 16)))
    exponents = with_ends(jax.random.randint(key_of[4], (3, D // QB, SEQ // QB), -2, 2), jax.random.fold_in(key_of[4], 1), -2, 1).astype(jnp.int32)
    filter_taps = draw_filter_taps(jax.random.fold_in(key_of[6], 71), 0)
    return dict(q_vals=q_vals, k_vals=k_vals, v_vals=v_vals, grad_out=grad_out, exponents=exponents, filter_taps=filter_taps)


EPS = 1e-6


def reference(q_vals, k_vals, v_vals, grad_out, exponents, filter_taps):
    group_width = D // FILTER_GROUPS
    slab_width = D // 16
    slab_groups = FILTER_GROUPS // 16
    scales = jnp.exp2(exponents.astype(jnp.float32))
    scales = scales.reshape(3, 16, slab_width // QB, SEQ // QB).transpose(1, 0, 2, 3)
    taps = lax.optimization_barrier(filter_taps.astype(jnp.bfloat16)).astype(jnp.float32)
    padded = jnp.pad(taps, ((0, 0), (0, SEQ - FILTER_TAP_COUNT))).reshape(16, slab_groups, SEQ)

    def expand(scale):
        return jnp.repeat(jnp.repeat(scale, QB, axis=0), QB, axis=1)

    def one_slab(pieces):
        q_part, k_part, v_part, g_part, scale_part, tap_part = pieces
        q_real = q_part.astype(jnp.float32) * expand(scale_part[0])
        k_real = k_part.astype(jnp.float32) * expand(scale_part[1])
        v_real = v_part.astype(jnp.float32) * expand(scale_part[2])
        gated = lax.optimization_barrier((k_real * v_real).astype(jnp.bfloat16)).astype(jnp.float32)
        grad_mix = lax.optimization_barrier((q_real * g_part.astype(jnp.float32)).astype(jnp.bfloat16)).astype(jnp.float32)
        per_channel = jnp.repeat(tap_part, group_width, axis=0)
        z_freq = jnp.fft.rfft(gated, axis=1)
        h_freq = jnp.fft.rfft(per_channel, axis=1)
        g_freq = jnp.fft.rfft(grad_mix, axis=1)
        conv_out = jnp.fft.irfft(z_freq * h_freq, n=SEQ, axis=1)
        grad_z = jnp.fft.irfft(g_freq * jnp.conj(h_freq), n=SEQ, axis=1)
        correl = jnp.fft.irfft(g_freq * jnp.conj(z_freq), n=SEQ, axis=1)
        grad_taps = correl.reshape(slab_groups, group_width, SEQ).sum(axis=1)[:, :FILTER_TAP_COUNT]
        grad_gate = g_part.astype(jnp.float32) * conv_out
        return grad_gate, grad_z * v_real, grad_z * k_real, grad_taps

    grad_gate, grad_key, grad_value, grad_taps = lax.map(
        one_slab,
        (q_vals.reshape(16, slab_width, SEQ), k_vals.reshape(16, slab_width, SEQ),
         v_vals.reshape(16, slab_width, SEQ), grad_out.reshape(16, slab_width, SEQ),
         scales, padded))
    grad_gate = grad_gate.reshape(D, SEQ)
    grad_key = grad_key.reshape(D, SEQ)
    grad_value = grad_value.reshape(D, SEQ)
    grad_filter = grad_taps.reshape(FILTER_GROUPS, FILTER_TAP_COUNT)

    def block_max(values):
        return jnp.max(jnp.abs(values).reshape(D, SEQ // QB, QB), axis=(0, 2))

    grad_amax = jnp.stack([block_max(grad_gate), block_max(grad_key), block_max(grad_value)])

    def scaled(values, peak):
        return (values / (jnp.repeat(peak, QB) + EPS)[None, :]).astype(jnp.bfloat16)

    return (scaled(grad_gate, grad_amax[0]), scaled(grad_key, grad_amax[1]),
            scaled(grad_value, grad_amax[2]), grad_filter, grad_amax)
```

```python
import functools

import jax
import jax.numpy as jnp
from jax import lax
from jax.experimental import pallas as pl
from jax.experimental.pallas import tpu as pltpu
from jax.sharding import PartitionSpec as P

WINDOW = 4
EPS = 1e-06
TILE = 128


def shift_by(shard, axis, by):
    devices = lax.axis_size(axis)
    return lax.ppermute(shard, axis, [(i, (i + by) % devices) for i in range(devices)])


def power(exponent):
    return lax.shift_left(jnp.int32(1), exponent + 8).astype(jnp.float32) * (2.0 ** -8)


def gate_kernel(e_ref, q_ref, k_ref, v_ref, g_ref, z_ref, gw_ref):
    b = pl.program_id(0)
    for r in range(q_ref.shape[1] // TILE):
        lanes = slice(r * TILE, (r + 1) * TILE)
        q_real = q_ref[:, lanes].astype(jnp.float32) * power(e_ref[0, b, r])
        k_real = k_ref[:, lanes].astype(jnp.float32) * power(e_ref[1, b, r])
        v_real = v_ref[:, lanes].astype(jnp.float32) * power(e_ref[2, b, r])
        z_ref[:, lanes] = (k_real * v_real).astype(jnp.bfloat16)
        gw_ref[:, lanes] = (q_real * g_ref[:, lanes].astype(jnp.float32)).astype(jnp.bfloat16)


def conv_kernel(e_ref, taps_ref, *refs, width, halo):
    zs = refs[: halo + 1]
    gws = refs[halo + 1 : 2 * halo + 2]
    k_ref, v_ref, g_ref, w_ref, gz_ref, lag_ref, peak_ref, toe_ref, corr_ref = refs[2 * halo + 2 :]
    b = pl.program_id(0)
    groups, taps = taps_ref.shape
    rows = w_ref.shape[1]
    parts = rows // TILE
    span = taps + TILE
    tiles = span // TILE

    @pl.when(b == 0)
    def _():
        peak_ref[...] = jnp.zeros(peak_ref.shape, jnp.float32)

    def one_group(g, carry):
        at = pl.ds(pl.multiple_of(g * width, width), width)
        row = taps_ref[pl.ds(g, 1), :].astype(jnp.bfloat16).astype(jnp.float32)
        row = jnp.concatenate([row, jnp.zeros((1, TILE), jnp.float32)], axis=1)
        base = pltpu.roll(jnp.broadcast_to(row, (8, span)), 0, 1, stride=1, stride_axis=0)
        for a in range(0, TILE, 16):
            low = pltpu.roll(base, a, 1) if a else base
            high = pltpu.roll(base, a + 8, 1)
            toe_ref[a : a + 16, :] = jnp.concatenate([low, high], axis=0).astype(jnp.bfloat16)
        z_all = jnp.concatenate([ref[at, :] for ref in reversed(zs)], axis=1)
        gw_all = jnp.concatenate([ref[at, :] for ref in gws], axis=1)
        z_win = jnp.concatenate(
            [
                jnp.concatenate(
                    [z_all[:, (p + tiles - 1 - d) * TILE : (p + tiles - d) * TILE] for d in range(tiles)],
                    axis=1,
                )
                for p in range(parts)
            ],
            axis=0,
        )
        gw_win = jnp.concatenate(
            [gw_all[:, p * TILE : p * TILE + span] for p in range(parts)], axis=0
        )
        stacked = jnp.concatenate(
            [toe_ref[:, d * TILE : (d + 1) * TILE] for d in range(tiles)], axis=0
        )
        w = jnp.dot(z_win, stacked, preferred_element_type=jnp.float32)
        gz = lax.dot_general(
            gw_win, toe_ref[...], (((1,), (1,)), ((), ())), preferred_element_type=jnp.float32
        )
        z_own = z_all[:, taps : taps + rows]
        z_loc = jnp.concatenate([z_own[:, p * TILE : (p + 1) * TILE] for p in range(parts)], axis=0)
        corr_ref[...] = lax.dot_general(
            z_loc, gw_win, (((0,), (0,)), ((), ())), preferred_element_type=jnp.float32
        )
        fold = TILE // 2
        held = corr_ref[0:fold, :] + pltpu.roll(corr_ref[fold : 2 * fold, :], span - fold, 1)
        while fold > 1:
            fold //= 2
            held = held[0:fold, :] + pltpu.roll(held[fold : 2 * fold, :], span - fold, 1)
        lag_ref[pl.ds(g, 1), :] = held[:, :taps]
        for p in range(parts):
            lanes = slice(p * TILE, (p + 1) * TILE)
            w_p = w[p * width : (p + 1) * width, :]
            gz_p = gz[p * width : (p + 1) * width, :]
            w_ref[at, lanes] = w_p
            gz_ref[at, lanes] = gz_p
            products = (
                g_ref[at, lanes].astype(jnp.float32) * w_p,
                gz_p * (v_ref[at, lanes].astype(jnp.float32) * power(e_ref[2, b, p])),
                gz_p * (k_ref[at, lanes].astype(jnp.float32) * power(e_ref[1, b, p])),
            )
            for i, product in enumerate(products):
                top = jnp.max(jnp.abs(product), axis=0, keepdims=True)
                spot = slice(p * 4 + i, p * 4 + i + 1)
                peak_ref[spot, :] = jnp.maximum(peak_ref[spot, :], top)
        return carry

    lax.fori_loop(0, groups, one_group, 0)


def scale_kernel(e_ref, peak_ref, k_ref, v_ref, g_ref, w_ref, gz_ref, oq_ref, ok_ref, ov_ref):
    b = pl.program_id(0)
    for p in range(w_ref.shape[1] // TILE):
        lanes = slice(p * TILE, (p + 1) * TILE)
        inverse = 1.0 / (peak_ref[...] + EPS)
        w = w_ref[:, lanes]
        gz = gz_ref[:, lanes]
        oq_ref[:, lanes] = (
            g_ref[:, lanes].astype(jnp.float32) * w * inverse[p * 4 : p * 4 + 1, :]
        ).astype(jnp.bfloat16)
        v_real = v_ref[:, lanes].astype(jnp.float32) * power(e_ref[2, b, p])
        k_real = k_ref[:, lanes].astype(jnp.float32) * power(e_ref[1, b, p])
        ok_ref[:, lanes] = (gz * v_real * inverse[p * 4 + 1 : p * 4 + 2, :]).astype(jnp.bfloat16)
        ov_ref[:, lanes] = (gz * k_real * inverse[p * 4 + 2 : p * 4 + 3, :]).astype(jnp.bfloat16)


def shards(q_vals, k_vals, v_vals, grad_out, exponents, filter_taps):
    channels, rows = q_vals.shape
    groups, taps = filter_taps.shape
    blocks = exponents.shape[1]
    block = channels // blocks
    width = channels // groups
    halo = taps // rows
    steps = (blocks,)
    scalars = pl.BlockSpec(memory_space=pltpu.SMEM)
    tile = pl.BlockSpec((block, rows), lambda b: (b, 0))
    whole = pl.BlockSpec((8, TILE), lambda b: (0, 0))
    shape = lambda dtype: jax.ShapeDtypeStruct((channels, rows), dtype)

    z, gw = pl.pallas_call(
        gate_kernel,
        grid=steps,
        in_specs=[scalars] + [tile] * 4,
        out_specs=[tile] * 2,
        out_shape=[shape(jnp.bfloat16)] * 2,
        name="gate",
    )(exponents, q_vals, k_vals, v_vals, grad_out)

    zs = [z]
    gws = [gw]
    for _ in range(halo):
        zs.append(shift_by(zs[-1], "ctx", 1))
        gws.append(shift_by(gws[-1], "ctx", -1))

    per_block = groups // blocks
    lag_block = pl.BlockSpec((per_block, taps), lambda b: (b, 0))
    w, gz, lag, peak = pl.pallas_call(
        functools.partial(conv_kernel, width=width, halo=halo),
        grid=steps,
        in_specs=[scalars, lag_block] + [tile] * (2 * halo + 2 + 3),
        out_specs=[tile, tile, lag_block, whole],
        out_shape=[
            shape(jnp.float32),
            shape(jnp.float32),
            jax.ShapeDtypeStruct((groups, taps), jnp.float32),
            jax.ShapeDtypeStruct((8, TILE), jnp.float32),
        ],
        scratch_shapes=[
            pltpu.VMEM((TILE, taps + TILE), jnp.bfloat16),
            pltpu.VMEM((TILE, taps + TILE), jnp.float32),
        ],
        name="conv",
    )(exponents, filter_taps, *zs, *gws, k_vals, v_vals, grad_out)

    ch = lax.axis_size("ch")
    peak_all = lax.all_to_all(
        jnp.broadcast_to(peak, (ch, 8, TILE)), "ch", split_axis=0, concat_axis=0, tiled=True
    )
    peak = jnp.broadcast_to(jnp.max(peak_all, axis=(0, 2))[:, None], (8, TILE))

    oq, ok, ov = pl.pallas_call(
        scale_kernel,
        grid=steps,
        in_specs=[scalars, whole] + [tile] * 5,
        out_specs=[tile] * 3,
        out_shape=[shape(jnp.bfloat16)] * 3,
        name="scale",
    )(exponents, peak, k_vals, v_vals, grad_out, w, gz)

    ctx = lax.axis_size("ctx")
    pieces = lax.all_to_all(
        lag.reshape(groups, ctx, taps // ctx).transpose(1, 0, 2), "ctx", split_axis=0, concat_axis=0, tiled=True
    )
    grad_filter = jnp.sum(pieces, axis=0)
    block_peak = peak[:, 0].reshape(2, 4)[:, :3].T
    return oq, ok, ov, grad_filter, block_peak


def solution(mesh):
    in_specs = (
        P("ch", "ctx"),
        P("ch", "ctx"),
        P("ch", "ctx"),
        P("ch", "ctx"),
        P(None, "ch", "ctx"),
        P("ch", None),
    )
    out_specs = (P("ch", "ctx"), P("ch", "ctx"), P("ch", "ctx"), P("ch", "ctx"), P(None, "ctx"))
    return jax.shard_map(shards, mesh=mesh, in_specs=in_specs, out_specs=out_specs, check_vma=False)
```

```python
import functools

import jax
import jax.numpy as jnp
from jax import lax
from jax.experimental import pallas as pl
from jax.experimental.pallas import tpu as pltpu
from jax.sharding import PartitionSpec as P

WINDOW = 4
EPS = 1e-06
TILE = 128
FINE = 32
UNROLL = 4


def shift_by(shard, axis, by):
    devices = lax.axis_size(axis)
    return lax.ppermute(shard, axis, [(i, (i + by) % devices) for i in range(devices)])


def power(exponent):
    return lax.shift_left(jnp.int32(1), exponent + 8).astype(jnp.float32) * (2.0 ** -8)


def mirror():
    shape = (TILE, TILE)
    rows = lax.broadcasted_iota(jnp.int32, shape, 0)
    lanes = lax.broadcasted_iota(jnp.int32, shape, 1)
    return (rows + lanes == TILE - 1).astype(jnp.float32).astype(jnp.bfloat16)


def mirrored(values, flip, terms):
    pieces = []
    rest = values
    for _ in range(terms):
        piece = rest.astype(jnp.bfloat16)
        pieces.append(piece)
        rest = rest - piece.astype(jnp.float32)
    return jnp.dot(
        jnp.concatenate(pieces, axis=1),
        jnp.concatenate([flip] * terms, axis=0),
        preferred_element_type=jnp.float32,
    )


def gate_kernel(e_ref, q_ref, k_ref, v_ref, g_ref, z_ref, back_ref):
    b = pl.program_id(0)
    flip = mirror()
    parts = q_ref.shape[1] // TILE
    for r in range(parts):
        lanes = slice(r * TILE, (r + 1) * TILE)
        other = slice((parts - 1 - r) * TILE, (parts - r) * TILE)
        q_real = q_ref[:, lanes].astype(jnp.float32) * power(e_ref[0, b, r])
        k_real = k_ref[:, lanes].astype(jnp.float32) * power(e_ref[1, b, r])
        v_real = v_ref[:, lanes].astype(jnp.float32) * power(e_ref[2, b, r])
        z_ref[:, lanes] = (k_real * v_real).astype(jnp.bfloat16)
        gw = (q_real * g_ref[:, lanes].astype(jnp.float32)).astype(jnp.bfloat16)
        back_ref[:, other] = jnp.dot(gw, flip, preferred_element_type=jnp.float32).astype(jnp.bfloat16)


def conv_kernel(e_ref, taps_ref, *refs, width, halo, first):
    zs = refs[: halo + 1]
    backs = refs[halo + 1 : 2 * halo + 2]
    k_ref, v_ref, g_ref, w_ref, gz_ref, lag_ref, peak_ref, turn_ref, diag_ref, *toe_refs = refs[2 * halo + 2 :]
    step = pl.program_id(0)
    b = step + first
    groups, taps = taps_ref.shape
    rows = w_ref.shape[1]
    parts = rows // TILE
    span = taps + TILE
    tiles = span // TILE

    @pl.when(step == 0)
    def _():
        peak_ref[...] = jnp.zeros(peak_ref.shape, jnp.float32)

    def windows(everything):
        return [
            jnp.concatenate(
                [
                    everything[:, (p + tiles - 1 - d) * TILE : (p + tiles - d) * TILE]
                    for d in range(tiles)
                ],
                axis=1,
            )
            for p in range(parts)
        ]

    def one_group(g, toe_ref):
        at = pl.ds(pl.multiple_of(g * width, width), width)
        row = taps_ref[pl.ds(g, 1), :].astype(jnp.bfloat16).astype(jnp.float32)
        row = jnp.concatenate([row, jnp.zeros((1, TILE), jnp.float32)], axis=1)
        row = jnp.broadcast_to(row, (8, span))
        low = pltpu.roll(row, 0, 1, stride=1, stride_axis=0)
        high = pltpu.roll(row, 8, 1, stride=1, stride_axis=0)
        base = jnp.concatenate([low, high], axis=0).astype(jnp.bfloat16)
        for a in range(0, TILE, 16):
            rolled = pltpu.roll(base, a, 1) if a else base
            for d in range(tiles):
                toe_ref[d * TILE + a : d * TILE + a + 16, :] = rolled[:, d * TILE : (d + 1) * TILE]
        z_all = jnp.concatenate([ref[at, :] for ref in reversed(zs)], axis=1)
        back_all = jnp.concatenate([ref[at, :] for ref in reversed(backs)], axis=1)
        sources = jnp.concatenate(windows(z_all) + windows(back_all), axis=0)
        both = jnp.dot(sources, toe_ref[...], preferred_element_type=jnp.float32)
        for p in range(parts):
            lanes = slice(p * TILE, (p + 1) * TILE)
            w_ref[at, lanes] = both[p * width : (p + 1) * width, :]
            turn_ref[at, lanes] = both[(parts + p) * width : (parts + p + 1) * width, :]
        back_own = back_all[:, taps : taps + rows]
        own_parts = []
        z_parts = []
        for m in range(TILE // FINE):
            z_m = pltpu.roll(z_all, taps + rows - m * FINE, 1) if m else z_all
            n = TILE // FINE - 1 - m
            back_n = pltpu.roll(back_own, rows - n * FINE, 1) if n else back_own
            for p in range(parts):
                z_parts.append(z_m[:, p * TILE : p * TILE + span])
                o = parts - 1 - p
                own_parts.append(back_n[:, o * TILE : (o + 1) * TILE])
        cross = lax.dot_general(
            jnp.concatenate(own_parts, axis=0),
            jnp.concatenate(z_parts, axis=0),
            (((0,), (0,)), ((), ())),
            preferred_element_type=jnp.float32,
        )
        total = None
        for a in range(0, FINE, 8):
            turned = pltpu.roll(
                cross[a : a + 8, :], (a + span - FINE) % span, 1, stride=1, stride_axis=0
            )
            total = turned if total is None else total + turned
        diag_ref[pl.ds(g, 1), :] = jnp.sum(total, axis=0, keepdims=True)[:, :taps]

    def some_groups(n, carry):
        for u in range(UNROLL):
            one_group(n * UNROLL + u, toe_refs[u])
        return carry

    lax.fori_loop(0, groups // UNROLL, some_groups, 0)

    flip = mirror()
    diag = diag_ref[...]
    blocks = taps // TILE
    stacked = jnp.concatenate([diag[:, n * TILE : (n + 1) * TILE] for n in range(blocks)], axis=0)
    stacked = mirrored(stacked, flip, 3)
    for n in range(blocks):
        o = blocks - 1 - n
        lag_ref[:, o * TILE : (o + 1) * TILE] = stacked[n * groups : (n + 1) * groups, :]
    for p in range(parts):
        o = parts - 1 - p
        lanes = slice(p * TILE, (p + 1) * TILE)
        gz = mirrored(turn_ref[:, o * TILE : (o + 1) * TILE], flip, 3)
        gz_ref[:, lanes] = gz
        products = (
            g_ref[:, lanes].astype(jnp.float32) * w_ref[:, lanes],
            gz * (v_ref[:, lanes].astype(jnp.float32) * power(e_ref[2, b, p])),
            gz * (k_ref[:, lanes].astype(jnp.float32) * power(e_ref[1, b, p])),
        )
        for i, product in enumerate(products):
            top = jnp.max(jnp.abs(product), axis=0, keepdims=True)
            spot = slice(p * 4 + i, p * 4 + i + 1)
            peak_ref[spot, :] = jnp.maximum(peak_ref[spot, :], top)


def scale_kernel(e_ref, peak_ref, k_ref, v_ref, g_ref, w_ref, gz_ref, oq_ref, ok_ref, ov_ref):
    b = pl.program_id(0)
    for p in range(w_ref.shape[1] // TILE):
        lanes = slice(p * TILE, (p + 1) * TILE)
        inverse = 1.0 / (peak_ref[...] + EPS)
        w = w_ref[:, lanes]
        gz = gz_ref[:, lanes]
        oq_ref[:, lanes] = (
            g_ref[:, lanes].astype(jnp.float32) * w * inverse[p * 4 : p * 4 + 1, :]
        ).astype(jnp.bfloat16)
        v_real = v_ref[:, lanes].astype(jnp.float32) * power(e_ref[2, b, p])
        k_real = k_ref[:, lanes].astype(jnp.float32) * power(e_ref[1, b, p])
        ok_ref[:, lanes] = (gz * v_real * inverse[p * 4 + 1 : p * 4 + 2, :]).astype(jnp.bfloat16)
        ov_ref[:, lanes] = (gz * k_real * inverse[p * 4 + 2 : p * 4 + 3, :]).astype(jnp.bfloat16)


def shards(q_vals, k_vals, v_vals, grad_out, exponents, filter_taps):
    channels, rows = q_vals.shape
    groups, taps = filter_taps.shape
    blocks = exponents.shape[1]
    block = channels // blocks
    width = channels // groups
    halo = taps // rows
    steps = (blocks,)
    scalars = pl.BlockSpec(memory_space=pltpu.SMEM)
    tile = pl.BlockSpec((block, rows), lambda b: (b, 0))
    whole = pl.BlockSpec((8, TILE), lambda b: (0, 0))
    shape = lambda dtype: jax.ShapeDtypeStruct((channels, rows), dtype)

    z, back = pl.pallas_call(
        gate_kernel,
        grid=steps,
        in_specs=[scalars] + [tile] * 4,
        out_specs=[tile] * 2,
        out_shape=[shape(jnp.bfloat16)] * 2,
        name="gate",
    )(exponents, q_vals, k_vals, v_vals, grad_out)

    zs = [z]
    backs = [back]
    for _ in range(halo):
        zs.append(shift_by(zs[-1], "ctx", 1))
        backs.append(shift_by(backs[-1], "ctx", -1))

    per_block = groups // blocks
    lag_block = pl.BlockSpec((per_block, taps), lambda b: (b, 0))
    w, gz, lag, peak = pl.pallas_call(
        functools.partial(conv_kernel, width=width, halo=halo, first=0),
        grid=steps,
        in_specs=[scalars, lag_block] + [tile] * (2 * halo + 2 + 3),
        out_specs=[tile, tile, lag_block, whole],
        out_shape=[
            shape(jnp.float32),
            shape(jnp.float32),
            jax.ShapeDtypeStruct((groups, taps), jnp.float32),
            jax.ShapeDtypeStruct((8, TILE), jnp.float32),
        ],
        scratch_shapes=[
            pltpu.VMEM((block, rows), jnp.float32),
            pltpu.VMEM((per_block, taps), jnp.float32),
        ]
        + [pltpu.VMEM((taps + TILE, TILE), jnp.bfloat16)] * UNROLL,
        name="conv",
    )(exponents, filter_taps, *zs, *backs, k_vals, v_vals, grad_out)

    ch = lax.axis_size("ch")
    peak_all = lax.all_to_all(
        jnp.broadcast_to(peak, (ch, 8, TILE)), "ch", split_axis=0, concat_axis=0, tiled=True
    )
    peak = jnp.broadcast_to(jnp.max(peak_all, axis=(0, 2))[:, None], (8, TILE))

    oq, ok, ov = pl.pallas_call(
        scale_kernel,
        grid=steps,
        in_specs=[scalars, whole] + [tile] * 5,
        out_specs=[tile] * 3,
        out_shape=[shape(jnp.bfloat16)] * 3,
        name="scale",
    )(exponents, peak, k_vals, v_vals, grad_out, w, gz)

    ctx = lax.axis_size("ctx")
    pieces = lax.all_to_all(
        lag.reshape(groups, ctx, taps // ctx).transpose(1, 0, 2), "ctx", split_axis=0, concat_axis=0, tiled=True
    )
    grad_filter = jnp.sum(pieces, axis=0)
    block_peak = peak[:, 0].reshape(2, 4)[:, :3].T
    return oq, ok, ov, grad_filter, block_peak


def solution(mesh):
    in_specs = (
        P("ch", "ctx"),
        P("ch", "ctx"),
        P("ch", "ctx"),
        P("ch", "ctx"),
        P(None, "ch", "ctx"),
        P("ch", None),
    )
    out_specs = (P("ch", "ctx"), P("ch", "ctx"), P("ch", "ctx"), P("ch", "ctx"), P(None, "ctx"))
    return jax.shard_map(shards, mesh=mesh, in_specs=in_specs, out_specs=out_specs, check_vma=False)
```

```python
import functools

import jax
import jax.numpy as jnp
from jax import lax
from jax.experimental import pallas as pl
from jax.experimental.pallas import tpu as pltpu
from jax.sharding import PartitionSpec as P

EPS = 1e-06
TILE = 128


def power(exponent):
    return lax.shift_left(jnp.int32(1), exponent + 8).astype(jnp.float32) * (2.0 ** -8)


def mirror():
    shape = (TILE, TILE)
    rows = lax.broadcasted_iota(jnp.int32, shape, 0)
    lanes = lax.broadcasted_iota(jnp.int32, shape, 1)
    return (rows + lanes == TILE - 1).astype(jnp.float32).astype(jnp.bfloat16)


def mirrored(values, flip, terms):
    pieces = []
    rest = values
    for _ in range(terms):
        piece = rest.astype(jnp.bfloat16)
        pieces.append(piece)
        rest = rest - piece.astype(jnp.float32)
    return jnp.dot(
        jnp.concatenate(pieces, axis=1),
        jnp.concatenate([flip] * terms, axis=0),
        preferred_element_type=jnp.float32,
    )


def squares(ref, block):
    for n in range(ref.shape[0] // block):
        for p in range(PARTS):
            yield n, p, slice(n * block, (n + 1) * block), slice(p * TILE, (p + 1) * TILE)


PARTS = 2


def gate_kernel(e_ref, q_ref, k_ref, v_ref, g_ref, out_ref, *, block):
    first = pl.program_id(0) * (q_ref.shape[0] // block)
    flip = mirror()
    for n, p, at, lanes in squares(q_ref, block):
        b = first + n
        q_real = q_ref[at, lanes].astype(jnp.float32) * power(e_ref[0, b, p])
        k_real = k_ref[at, lanes].astype(jnp.float32) * power(e_ref[1, b, p])
        v_real = v_ref[at, lanes].astype(jnp.float32) * power(e_ref[2, b, p])
        out_ref[at, lanes] = (k_real * v_real).astype(jnp.bfloat16)
        gw = (q_real * g_ref[at, lanes].astype(jnp.float32)).astype(jnp.bfloat16)
        o = 2 * PARTS - 1 - p
        out_ref[at, o * TILE : (o + 1) * TILE] = jnp.dot(
            gw, flip, preferred_element_type=jnp.float32
        ).astype(jnp.bfloat16)


def conv_kernel(taps_ref, x_ref, y_ref, lag_ref, toe_ref, z_ref, u_ref, b_ref):
    blocks, width = x_ref.shape[:2]
    taps = taps_ref.shape[2]
    span = taps + TILE
    tiles = span // TILE
    lead = tiles - 1
    count = blocks * PARTS

    row = taps_ref[0].astype(jnp.bfloat16).astype(jnp.float32)
    row = jnp.concatenate([row, jnp.zeros((1, TILE), jnp.float32)], axis=1)
    row = jnp.broadcast_to(row, (8, span))
    low = pltpu.roll(row, 0, 1, stride=1, stride_axis=0)
    high = pltpu.roll(row, 8, 1, stride=1, stride_axis=0)
    base = jnp.concatenate([low, high], axis=0).astype(jnp.bfloat16)
    for a in range(0, TILE, 16):
        rolled = pltpu.roll(base, a, 1) if a else base
        for d in range(tiles):
            toe_ref[d * TILE + a : d * TILE + a + 16, :] = rolled[:, d * TILE : (d + 1) * TILE]

    def z_tile(t):
        t = t % count
        return x_ref[t // PARTS, :, (t % PARTS) * TILE : (t % PARTS + 1) * TILE]

    def back_tile(t):
        t = t % count
        o = PARTS + t % PARTS
        return x_ref[blocks - 1 - t // PARTS, :, o * TILE : (o + 1) * TILE]

    for n in range(count + lead):
        rows = slice(n * width, (n + 1) * width)
        z_ref[rows, :] = z_tile(n - lead)
        b_ref[rows, :] = back_tile(n - lead)
        u_ref[rows, :] = z_tile(count - 1 - n)

    def window(ref):
        return jnp.concatenate(
            [ref[(lead - d) * width : (lead - d + count) * width, :] for d in range(tiles)], axis=1
        )

    w = jnp.dot(window(z_ref), toe_ref[...], preferred_element_type=jnp.float32)
    for t in range(count):
        y_ref[t // PARTS, :, (t % PARTS) * TILE : (t % PARTS + 1) * TILE] = w[
            t * width : (t + 1) * width, :
        ].astype(jnp.bfloat16)
    gz = jnp.dot(window(b_ref), toe_ref[...], preferred_element_type=jnp.float32)
    for t in range(count):
        o = PARTS + t % PARTS
        y_ref[blocks - 1 - t // PARTS, :, o * TILE : (o + 1) * TILE] = gz[
            t * width : (t + 1) * width, :
        ].astype(jnp.bfloat16)

    cross = lax.dot_general(
        b_ref[lead * width : (lead + count) * width, :],
        window(u_ref),
        (((0,), (0,)), ((), ())),
        preferred_element_type=jnp.float32,
    )
    total = None
    for a in range(0, TILE, 8):
        turned = pltpu.roll(
            cross[a : a + 8, :], (a + span - TILE) % span, 1, stride=1, stride_axis=0
        )
        total = turned if total is None else total + turned
    diag = jnp.sum(total, axis=0, keepdims=True)
    pieces = taps // TILE
    stacked = jnp.concatenate([diag[:, n * TILE : (n + 1) * TILE] for n in range(pieces)], axis=0)
    stacked = mirrored(stacked, mirror(), 3)
    for n in range(pieces):
        o = pieces - 1 - n
        lag_ref[0, o : o + 1, :] = stacked[n : n + 1, :]


def gradients(e_ref, k_ref, v_ref, g_ref, y_ref, block):
    first = pl.program_id(0) * (k_ref.shape[0] // block)
    flip = mirror()
    for n, p, at, lanes in squares(k_ref, block):
        o = 2 * PARTS - 1 - p
        w = y_ref[at, lanes].astype(jnp.float32)
        gz = jnp.dot(
            y_ref[at, o * TILE : (o + 1) * TILE], flip, preferred_element_type=jnp.float32
        )
        v_real = v_ref[at, lanes].astype(jnp.float32) * power(e_ref[2, first + n, p])
        k_real = k_ref[at, lanes].astype(jnp.float32) * power(e_ref[1, first + n, p])
        g = g_ref[at, lanes].astype(jnp.float32)
        yield p, at, lanes, (g * w, gz * v_real, gz * k_real)


def peak_kernel(e_ref, k_ref, v_ref, g_ref, y_ref, peak_ref, *, block):
    @pl.when(pl.program_id(0) == 0)
    def _():
        peak_ref[...] = jnp.zeros(peak_ref.shape, jnp.float32)

    for p, at, lanes, products in gradients(e_ref, k_ref, v_ref, g_ref, y_ref, block):
        for i, product in enumerate(products):
            top = jnp.max(jnp.abs(product), axis=0, keepdims=True)
            spot = slice(p * 4 + i, p * 4 + i + 1)
            peak_ref[spot, :] = jnp.maximum(peak_ref[spot, :], top)

    @pl.when(pl.program_id(0) == pl.num_programs(0) - 1)
    def _():
        best = jnp.max(peak_ref[...], axis=1, keepdims=True)
        peak_ref[...] = jnp.broadcast_to(best, peak_ref.shape)


def scale_kernel(e_ref, k_ref, v_ref, g_ref, y_ref, *refs, block):
    peaks, (oq_ref, ok_ref, ov_ref, top_ref) = refs[:-4], refs[-4:]
    top = peaks[0][...]
    for ref in peaks[1:]:
        top = jnp.maximum(top, ref[...])
    top_ref[...] = top
    inverse = 1.0 / (top + EPS)
    for p, at, lanes, products in gradients(e_ref, k_ref, v_ref, g_ref, y_ref, block):
        for i, (product, ref) in enumerate(zip(products, (oq_ref, ok_ref, ov_ref))):
            ref[at, lanes] = (product * inverse[p * 4 + i : p * 4 + i + 1, :]).astype(jnp.bfloat16)


def shards(q_vals, k_vals, v_vals, grad_out, exponents, filter_taps):
    channels, rows = q_vals.shape
    groups, taps = filter_taps.shape
    block = channels // exponents.shape[1]
    width = channels // groups
    ctx = lax.axis_size("ctx")
    ch = lax.axis_size("ch")
    part = channels // ctx
    mine = groups // ctx
    span = taps + TILE
    tall = 2 * block
    steps = (channels // tall,)
    scalars = pl.BlockSpec(memory_space=pltpu.SMEM)
    tile = pl.BlockSpec((tall, rows), lambda b: (b, 0))
    double = pl.BlockSpec((tall, 2 * rows), lambda b: (b, 0))
    whole = pl.BlockSpec((8, TILE), lambda b: (0, 0))
    bf16 = jnp.bfloat16

    gated = pl.pallas_call(
        functools.partial(gate_kernel, block=block),
        grid=steps,
        in_specs=[scalars] + [tile] * 4,
        out_specs=double,
        out_shape=jax.ShapeDtypeStruct((channels, 2 * rows), bf16),
        name="gate",
    )(exponents, q_vals, k_vals, v_vals, grad_out)
    swapped = lax.all_to_all(gated, "ctx", split_axis=0, concat_axis=0, tiled=True)

    own_taps = lax.dynamic_slice_in_dim(filter_taps, lax.axis_index("ctx") * mine, mine, 0)
    stack = pltpu.VMEM(((ctx * PARTS + taps // TILE) * width, TILE), bf16)
    seq = pl.BlockSpec((ctx, width, 2 * rows), lambda b: (0, b, 0))
    y, lag = pl.pallas_call(
        conv_kernel,
        grid=(mine,),
        in_specs=[pl.BlockSpec((1, 1, taps), lambda b: (b, 0, 0)), seq],
        out_specs=[seq, pl.BlockSpec((1, taps // TILE, TILE), lambda b: (b, 0, 0))],
        out_shape=[
            jax.ShapeDtypeStruct((ctx, part, 2 * rows), bf16),
            jax.ShapeDtypeStruct((mine, taps // TILE, TILE), jnp.float32),
        ],
        scratch_shapes=[pltpu.VMEM((span, TILE), bf16), stack, stack, stack],
        name="conv",
    )(own_taps.reshape(mine, 1, taps), swapped.reshape(ctx, part, 2 * rows))

    y = lax.all_to_all(y.reshape(channels, 2 * rows), "ctx", split_axis=0, concat_axis=0, tiled=True)
    pieces = lag.reshape(mine, ctx, taps // ctx).transpose(1, 0, 2)
    pieces = lax.all_to_all(pieces, "ctx", split_axis=0, concat_axis=0, tiled=True)
    grad_filter = pieces.reshape(groups, taps // ctx)

    peak = pl.pallas_call(
        functools.partial(peak_kernel, block=block),
        grid=steps,
        in_specs=[scalars] + [tile] * 3 + [double],
        out_specs=whole,
        out_shape=jax.ShapeDtypeStruct((8, TILE), jnp.float32),
        name="peak",
    )(exponents, k_vals, v_vals, grad_out, y)
    peaks = [peak]
    for by in range(1, ch):
        peaks.append(lax.ppermute(peak, "ch", [(i, (i + by) % ch) for i in range(ch)]))

    oq, ok, ov, top = pl.pallas_call(
        functools.partial(scale_kernel, block=block),
        grid=steps,
        in_specs=[scalars] + [tile] * 3 + [double] + [whole] * ch,
        out_specs=[tile] * 3 + [whole],
        out_shape=[jax.ShapeDtypeStruct((channels, rows), bf16)] * 3
        + [jax.ShapeDtypeStruct((8, TILE), jnp.float32)],
        name="scale",
    )(exponents, k_vals, v_vals, grad_out, y, *peaks)
    block_peak = top[:, 0].reshape(PARTS, 4)[:, :3].T
    return oq, ok, ov, grad_filter, block_peak


def solution(mesh):
    in_specs = (
        P("ch", "ctx"),
        P("ch", "ctx"),
        P("ch", "ctx"),
        P("ch", "ctx"),
        P(None, "ch", "ctx"),
        P("ch", None),
    )
    out_specs = (P("ch", "ctx"), P("ch", "ctx"), P("ch", "ctx"), P("ch", "ctx"), P(None, "ctx"))
    return jax.shard_map(shards, mesh=mesh, in_specs=in_specs, out_specs=out_specs, check_vma=False)
```

```python
import functools

import jax
import jax.numpy as jnp
from jax import lax
from jax.experimental import pallas as pl
from jax.experimental.pallas import tpu as pltpu
from jax.sharding import PartitionSpec as P

EPS = 1e-06
TILE = 128


def power(e_ref, i, b, p):
    exponent = e_ref[i]
    rows = lax.broadcasted_iota(jnp.int32, exponent.shape, 0)
    lanes = lax.broadcasted_iota(jnp.int32, exponent.shape, 1)
    value = lax.shift_left(jnp.ones_like(exponent), exponent + 8).astype(jnp.float32) * (2.0 ** -8)
    value = jnp.where((rows == p) & (lanes == b), value, 0.0)
    return jnp.sum(jnp.sum(value, axis=0, keepdims=True), axis=1, keepdims=True)


def mirror():
    shape = (TILE, TILE)
    rows = lax.broadcasted_iota(jnp.int32, shape, 0)
    lanes = lax.broadcasted_iota(jnp.int32, shape, 1)
    return (rows + lanes == TILE - 1).astype(jnp.float32).astype(jnp.bfloat16)


def mirrored(values, flip, terms):
    pieces = []
    rest = values
    for _ in range(terms):
        piece = rest.astype(jnp.bfloat16)
        pieces.append(piece)
        rest = rest - piece.astype(jnp.float32)
    return jnp.dot(
        jnp.concatenate(pieces, axis=1),
        jnp.concatenate([flip] * terms, axis=0),
        preferred_element_type=jnp.float32,
    )


def squares(ref, block):
    for n in range(ref.shape[0] // block):
        for p in range(PARTS):
            yield n, p, slice(n * block, (n + 1) * block), slice(p * TILE, (p + 1) * TILE)


PARTS = 2
TERMS = 3
EXTRA = 8


def gate_kernel(e_ref, q_ref, k_ref, v_ref, g_ref, out_ref, *, block):
    first = pl.program_id(0) * (q_ref.shape[0] // block)
    flip = mirror()
    for n, p, at, lanes in squares(q_ref, block):
        b = first + n
        q_real = q_ref[at, lanes].astype(jnp.float32) * power(e_ref, 0, b, p)
        k_real = k_ref[at, lanes].astype(jnp.float32) * power(e_ref, 1, b, p)
        v_real = v_ref[at, lanes].astype(jnp.float32) * power(e_ref, 2, b, p)
        out_ref[at, lanes] = (k_real * v_real).astype(jnp.bfloat16)
        gw = (q_real * g_ref[at, lanes].astype(jnp.float32)).astype(jnp.bfloat16)
        o = 2 * PARTS - 1 - p
        out_ref[at, o * TILE : (o + 1) * TILE] = jnp.dot(
            gw, flip, preferred_element_type=jnp.float32
        ).astype(jnp.bfloat16)


def conv_kernel(taps_ref, x_ref, y_ref, toe_ref, z_ref, u_ref, b_ref, lag_ref, *, width):
    blocks, part = x_ref.shape[:2]
    own = pl.ds(pl.multiple_of(pl.program_id(0) * width, width), width)
    taps = taps_ref.shape[2]
    span = taps + TILE
    tiles = span // TILE
    lead = tiles - 1
    count = blocks * PARTS

    row = taps_ref[0].astype(jnp.bfloat16).astype(jnp.float32)
    row = jnp.concatenate([row, jnp.zeros((1, TILE), jnp.float32)], axis=1)
    row = jnp.broadcast_to(row, (8, span))
    low = pltpu.roll(row, 0, 1, stride=1, stride_axis=0)
    high = pltpu.roll(row, 8, 1, stride=1, stride_axis=0)
    base = jnp.concatenate([low, high], axis=0).astype(jnp.bfloat16)
    for a in range(0, TILE, 16):
        rolled = pltpu.roll(base, a, 1) if a else base
        for d in range(tiles):
            toe_ref[d * TILE + a : d * TILE + a + 16, :] = rolled[:, d * TILE : (d + 1) * TILE]

    def z_tile(t):
        t = t % count
        return x_ref[t // PARTS, own, (t % PARTS) * TILE : (t % PARTS + 1) * TILE]

    def back_tile(t):
        t = t % count
        o = PARTS + t % PARTS
        return x_ref[blocks - 1 - t // PARTS, own, o * TILE : (o + 1) * TILE]

    for n in range(count + lead):
        rows = slice(n * width, (n + 1) * width)
        z_ref[rows, :] = z_tile(n - lead)
        b_ref[rows, :] = back_tile(n - lead)
        u_ref[rows, :] = z_tile(count - 1 - n)

    def window(ref):
        return jnp.concatenate(
            [ref[(lead - d) * width : (lead - d + count) * width, :] for d in range(tiles)], axis=1
        )

    w = jnp.dot(window(z_ref), toe_ref[...], preferred_element_type=jnp.float32)
    for t in range(count):
        y_ref[t // PARTS, own, (t % PARTS) * TILE : (t % PARTS + 1) * TILE] = w[
            t * width : (t + 1) * width, :
        ].astype(jnp.bfloat16)
    gz = jnp.dot(window(b_ref), toe_ref[...], preferred_element_type=jnp.float32)
    for t in range(count):
        o = PARTS + t % PARTS
        y_ref[blocks - 1 - t // PARTS, own, o * TILE : (o + 1) * TILE] = gz[
            t * width : (t + 1) * width, :
        ].astype(jnp.bfloat16)

    cross = lax.dot_general(
        b_ref[lead * width : (lead + count) * width, :],
        window(u_ref),
        (((0,), (0,)), ((), ())),
        preferred_element_type=jnp.float32,
    )
    total = None
    for a in range(0, TILE, 8):
        turned = pltpu.roll(
            cross[a : a + 8, :], (a + span - TILE) % span, 1, stride=1, stride_axis=0
        )
        total = turned if total is None else total + turned
    diag = jnp.sum(total, axis=0, keepdims=True)
    pieces = taps // TILE
    stacked = jnp.concatenate([diag[:, n * TILE : (n + 1) * TILE] for n in range(pieces)], axis=0)
    stacked = mirrored(stacked, mirror(), 3)
    share = lag_ref.shape[2]
    mine = pl.ds(pl.program_id(0), 1)
    for r in range(blocks):
        n = pieces - 1 - r * share // TILE
        at = r * share % TILE
        lag_ref[r, mine, :] = stacked[n : n + 1, at : at + share]

    @pl.when(pl.program_id(0) == 0)
    def _():
        y_ref[:, part:, :] = jnp.zeros((blocks, y_ref.shape[1] - part, y_ref.shape[2]), jnp.bfloat16)

    @pl.when(pl.program_id(0) == pl.num_programs(0) - 1)
    def _():
        rest = lag_ref[...]
        for term in range(TERMS):
            piece = rest.astype(jnp.bfloat16)
            y_ref[:, part : part + rest.shape[1], term * TILE : term * TILE + share] = piece
            rest = rest - piece.astype(jnp.float32)


def gradients(e_ref, k_ref, v_ref, g_ref, y_ref, block):
    first = pl.program_id(0) * (k_ref.shape[0] // block)
    part = y_ref.shape[1] - EXTRA
    each = block // part
    flip = mirror()
    for n, p, at, lanes in squares(k_ref, block):
        o = 2 * PARTS - 1 - p
        senders = range(n * each, (n + 1) * each)
        w = jnp.concatenate([y_ref[s, :part, lanes] for s in senders], axis=0).astype(jnp.float32)
        back = jnp.concatenate(
            [y_ref[s, :part, o * TILE : (o + 1) * TILE] for s in senders], axis=0
        )
        gz = jnp.dot(back, flip, preferred_element_type=jnp.float32)
        v_real = v_ref[at, lanes].astype(jnp.float32) * power(e_ref, 2, first + n, p)
        k_real = k_ref[at, lanes].astype(jnp.float32) * power(e_ref, 1, first + n, p)
        g = g_ref[at, lanes].astype(jnp.float32)
        yield p, at, lanes, (g * w, gz * v_real, gz * k_real)


def peak_kernel(e_ref, k_ref, v_ref, g_ref, y_ref, out_ref, peak_ref, *, block):
    @pl.when(pl.program_id(0) == 0)
    def _():
        peak_ref[...] = jnp.zeros(peak_ref.shape, jnp.float32)

    for p, at, lanes, products in gradients(e_ref, k_ref, v_ref, g_ref, y_ref, block):
        for i, product in enumerate(products):
            top = jnp.max(jnp.abs(product), axis=0, keepdims=True)
            spot = slice(p * 4 + i, p * 4 + i + 1)
            peak_ref[spot, :] = jnp.maximum(peak_ref[spot, :], top)

    @pl.when(pl.program_id(0) == pl.num_programs(0) - 1)
    def _():
        for n in range(out_ref.shape[0]):
            out_ref[n] = peak_ref[...]


def scale_kernel(e_ref, k_ref, v_ref, g_ref, y_ref, peaks_ref, oq_ref, ok_ref, ov_ref, lag_ref, top_ref, *, block):
    top = jnp.max(peaks_ref[...], axis=0)
    for p in range(PARTS):
        for i in range(3):
            best = jnp.max(top[p * 4 + i : p * 4 + i + 1, :], axis=1, keepdims=True)
            top_ref[p : p + 1, i : i + 1] = best
    top = jnp.max(top, axis=1, keepdims=True)
    part = y_ref.shape[1] - EXTRA
    share = lag_ref.shape[1]
    mine = lag_ref.shape[0] // y_ref.shape[0]
    for s in range(y_ref.shape[0]):
        terms = [
            y_ref[s, part:, t * TILE : t * TILE + share].astype(jnp.float32) for t in range(TERMS)
        ]
        lag_ref[s * mine : (s + 1) * mine, :] = (terms[0] + (terms[1] + terms[2]))[:mine, :]
    inverse = 1.0 / (top + EPS)
    for p, at, lanes, products in gradients(e_ref, k_ref, v_ref, g_ref, y_ref, block):
        for i, (product, ref) in enumerate(zip(products, (oq_ref, ok_ref, ov_ref))):
            ref[at, lanes] = (product * inverse[p * 4 + i : p * 4 + i + 1, :]).astype(jnp.bfloat16)


def shards(q_vals, k_vals, v_vals, grad_out, exponents, filter_taps):
    channels, rows = q_vals.shape
    groups, taps = filter_taps.shape
    block = channels // exponents.shape[1]
    width = channels // groups
    ctx = lax.axis_size("ctx")
    ch = lax.axis_size("ch")
    part = channels // ctx
    mine = groups // ctx
    span = taps + TILE
    tall = 2 * block
    steps = (channels // tall,)
    exponents = exponents.transpose(0, 2, 1)
    scalars = pl.BlockSpec(exponents.shape, lambda b: (0, 0, 0))
    tile = pl.BlockSpec((tall, rows), lambda b: (b, 0))
    double = pl.BlockSpec((tall, 2 * rows), lambda b: (b, 0))
    bf16 = jnp.bfloat16

    gated = pl.pallas_call(
        functools.partial(gate_kernel, block=block),
        grid=steps,
        in_specs=[scalars] + [tile] * 4,
        out_specs=double,
        out_shape=jax.ShapeDtypeStruct((channels, 2 * rows), bf16),
        name="gate",
    )(exponents, q_vals, k_vals, v_vals, grad_out)
    swapped = lax.all_to_all(gated, "ctx", split_axis=0, concat_axis=0, tiled=True)

    own_taps = lax.dynamic_slice_in_dim(filter_taps, lax.axis_index("ctx") * mine, mine, 0)
    stack = pltpu.VMEM(((ctx * PARTS + taps // TILE) * width, TILE), bf16)
    resident = pl.BlockSpec(memory_space=pltpu.VMEM)
    y = pl.pallas_call(
        functools.partial(conv_kernel, width=width),
        grid=(mine,),
        in_specs=[pl.BlockSpec((1, 1, taps), lambda b: (b, 0, 0)), resident],
        out_specs=resident,
        out_shape=jax.ShapeDtypeStruct((ctx, part + EXTRA, 2 * rows), bf16),
        scratch_shapes=[
            pltpu.VMEM((span, TILE), bf16),
            stack,
            stack,
            stack,
            pltpu.VMEM((ctx, EXTRA, taps // ctx), jnp.float32),
        ],
        name="conv",
    )(own_taps.reshape(mine, 1, taps), swapped.reshape(ctx, part, 2 * rows))

    y = lax.all_to_all(y, "ctx", split_axis=0, concat_axis=0, tiled=True)
    mixed = pl.BlockSpec((tall // part, part + EXTRA, 2 * rows), lambda b: (b, 0, 0))
    every = pl.BlockSpec((ch, 8, TILE), lambda b: (0, 0, 0))
    peaks = pl.pallas_call(
        functools.partial(peak_kernel, block=block),
        grid=steps,
        in_specs=[scalars] + [tile] * 3 + [mixed],
        out_specs=every,
        out_shape=jax.ShapeDtypeStruct((ch, 8, TILE), jnp.float32),
        scratch_shapes=[pltpu.VMEM((8, TILE), jnp.float32)],
        name="peak",
    )(exponents, k_vals, v_vals, grad_out, y)
    peaks = lax.all_to_all(peaks, "ch", split_axis=0, concat_axis=0, tiled=True)

    oq, ok, ov, grad_filter, top = pl.pallas_call(
        functools.partial(scale_kernel, block=block),
        grid=steps,
        in_specs=[scalars] + [tile] * 3 + [mixed, every],
        out_specs=[tile] * 3
        + [
            pl.BlockSpec((groups // steps[0], taps // ctx), lambda b: (b, 0)),
            pl.BlockSpec((PARTS, 3), lambda b: (0, 0)),
        ],
        out_shape=[jax.ShapeDtypeStruct((channels, rows), bf16)] * 3
        + [
            jax.ShapeDtypeStruct((groups, taps // ctx), jnp.float32),
            jax.ShapeDtypeStruct((PARTS, 3), jnp.float32),
        ],
        name="scale",
    )(exponents, k_vals, v_vals, grad_out, y, peaks)
    return oq, ok, ov, grad_filter, top.T


def solution(mesh):
    in_specs = (
        P("ch", "ctx"),
        P("ch", "ctx"),
        P("ch", "ctx"),
        P("ch", "ctx"),
        P(None, "ch", "ctx"),
        P("ch", None),
    )
    out_specs = (P("ch", "ctx"), P("ch", "ctx"), P("ch", "ctx"), P("ch", "ctx"), P(None, "ctx"))
    return jax.shard_map(shards, mesh=mesh, in_specs=in_specs, out_specs=out_specs, check_vma=False)
```

```python
import functools

import jax
import jax.numpy as jnp
from jax import lax
from jax.experimental import pallas as pl
from jax.experimental.pallas import tpu as pltpu
from jax.sharding import PartitionSpec as P

EPS = 1e-06
TILE = 128


def power(e_ref, i, b, p):
    exponent = e_ref[i]
    rows = lax.broadcasted_iota(jnp.int32, exponent.shape, 0)
    lanes = lax.broadcasted_iota(jnp.int32, exponent.shape, 1)
    value = lax.shift_left(jnp.ones_like(exponent), exponent + 8).astype(jnp.float32) * (2.0 ** -8)
    value = jnp.where((rows == p) & (lanes == b), value, 0.0)
    return jnp.sum(jnp.sum(value, axis=0, keepdims=True), axis=1, keepdims=True)


def mirror():
    shape = (TILE, TILE)
    rows = lax.broadcasted_iota(jnp.int32, shape, 0)
    lanes = lax.broadcasted_iota(jnp.int32, shape, 1)
    return (rows + lanes == TILE - 1).astype(jnp.float32).astype(jnp.bfloat16)


def mirrored(values, flip, terms):
    pieces = []
    rest = values
    for _ in range(terms):
        piece = rest.astype(jnp.bfloat16)
        pieces.append(piece)
        rest = rest - piece.astype(jnp.float32)
    return jnp.dot(
        jnp.concatenate(pieces, axis=1),
        jnp.concatenate([flip] * terms, axis=0),
        preferred_element_type=jnp.float32,
    )


def squares(ref, block):
    for n in range(ref.shape[0] // block):
        for p in range(PARTS):
            yield n, p, slice(n * block, (n + 1) * block), slice(p * TILE, (p + 1) * TILE)


PARTS = 2
TERMS = 3
EXTRA = 8


def gate_kernel(e_ref, q_ref, k_ref, v_ref, g_ref, out_ref, *, block):
    first = pl.program_id(0) * (q_ref.shape[0] // block)
    flip = mirror()
    for n, p, at, lanes in squares(q_ref, block):
        b = first + n
        q_real = q_ref[at, lanes].astype(jnp.float32) * power(e_ref, 0, b, p)
        k_real = k_ref[at, lanes].astype(jnp.float32) * power(e_ref, 1, b, p)
        v_real = v_ref[at, lanes].astype(jnp.float32) * power(e_ref, 2, b, p)
        out_ref[at, lanes] = (k_real * v_real).astype(jnp.bfloat16)
        gw = (q_real * g_ref[at, lanes].astype(jnp.float32)).astype(jnp.bfloat16)
        o = 2 * PARTS - 1 - p
        out_ref[at, o * TILE : (o + 1) * TILE] = jnp.dot(
            gw, flip, preferred_element_type=jnp.float32
        ).astype(jnp.bfloat16)


def conv_kernel(taps_ref, x_ref, y_ref, lag_ref, *scratch, width):
    blocks, part, lanes = x_ref.shape
    groups, taps = taps_ref.shape
    y_ref[:, part:, :] = jnp.zeros((blocks, y_ref.shape[1] - part, lanes), jnp.bfloat16)
    each = len(scratch) // groups
    for g in range(groups):
        one_group(g, taps_ref, x_ref, y_ref, lag_ref, *scratch[g * each : (g + 1) * each], width)
    rest = lag_ref[...]
    for term in range(TERMS):
        piece = rest.astype(jnp.bfloat16)
        y_ref[:, part : part + rest.shape[1], term * TILE : term * TILE + rest.shape[2]] = piece
        rest = rest - piece.astype(jnp.float32)


def one_group(g, taps_ref, x_ref, y_ref, lag_ref, toe_ref, z_ref, b_ref, own_ref, u_ref, width):
    blocks = x_ref.shape[0]
    taps = taps_ref.shape[1]
    span = taps + TILE
    tiles = span // TILE
    lead = tiles - 1
    count = blocks * PARTS
    own = slice(g * width, (g + 1) * width)

    row = taps_ref[g : g + 1, :].astype(jnp.bfloat16).astype(jnp.float32)
    row = jnp.concatenate([row, jnp.zeros((1, TILE), jnp.float32)], axis=1)
    row = jnp.broadcast_to(row, (8, span))
    low = pltpu.roll(row, 0, 1, stride=1, stride_axis=0)
    high = pltpu.roll(row, 8, 1, stride=1, stride_axis=0)
    base = jnp.concatenate([low, high], axis=0).astype(jnp.bfloat16)
    blank = jnp.zeros((TILE, TILE), jnp.bfloat16)
    toe_ref[0:TILE, 0:TILE] = blank
    toe_ref[tiles * TILE : (tiles + 1) * TILE, TILE : 2 * TILE] = blank
    for a in range(0, TILE, 16):
        rolled = pltpu.roll(base, a, 1) if a else base
        for d in range(tiles):
            piece = rolled[:, d * TILE : (d + 1) * TILE]
            toe_ref[(d + 1) * TILE + a : (d + 1) * TILE + a + 16, 0:TILE] = piece
            toe_ref[d * TILE + a : d * TILE + a + 16, TILE : 2 * TILE] = piece

    def z_tile(t):
        t = t % count
        return x_ref[t // PARTS, own, (t % PARTS) * TILE : (t % PARTS + 1) * TILE]

    def back_tile(t):
        t = t % count
        o = PARTS + t % PARTS
        return x_ref[blocks - 1 - t // PARTS, own, o * TILE : (o + 1) * TILE]

    half = lead // 2
    for m in range(blocks + half):
        rows = slice(m * width, (m + 1) * width)
        for p in range(2):
            lanes = slice((1 - p) * TILE, (2 - p) * TILE)
            z_ref[rows, lanes] = z_tile(2 * (m - half) + p)
            b_ref[rows, lanes] = back_tile(2 * (m - half) + p)
    for n in range(count):
        own_ref[n * width : (n + 1) * width, :] = back_tile(n)
    for n in range(count + lead):
        u_ref[n * width : (n + 1) * width, :] = z_tile(count - 1 - n)

    def window(ref):
        return jnp.concatenate(
            [ref[(half - f) * width : (half - f + blocks) * width, :] for f in range(half + 1)], axis=1
        )

    w = jnp.dot(window(z_ref), toe_ref[...], preferred_element_type=jnp.float32)
    for n in range(blocks):
        y_ref[n, own, 0 : 2 * TILE] = w[n * width : (n + 1) * width, :].astype(jnp.bfloat16)
    gz = jnp.dot(window(b_ref), toe_ref[...], preferred_element_type=jnp.float32)
    for n in range(blocks):
        y_ref[blocks - 1 - n, own, 2 * TILE : 4 * TILE] = gz[n * width : (n + 1) * width, :].astype(
            jnp.bfloat16
        )

    shifted = jnp.concatenate(
        [u_ref[(lead - d) * width : (lead - d + count) * width, :] for d in range(tiles)], axis=1
    )
    cross = lax.dot_general(
        own_ref[...], shifted, (((0,), (0,)), ((), ())), preferred_element_type=jnp.float32
    )
    total = None
    for a in range(0, TILE, 8):
        turned = pltpu.roll(
            cross[a : a + 8, :], (a + span - TILE) % span, 1, stride=1, stride_axis=0
        )
        total = turned if total is None else total + turned
    diag = jnp.sum(total, axis=0, keepdims=True)
    pieces = taps // TILE
    stacked = jnp.concatenate([diag[:, n * TILE : (n + 1) * TILE] for n in range(pieces)], axis=0)
    stacked = mirrored(stacked, mirror(), 3)
    share = lag_ref.shape[2]
    for r in range(blocks):
        n = pieces - 1 - r * share // TILE
        at = r * share % TILE
        lag_ref[r, g : g + 1, :] = stacked[n : n + 1, at : at + share]


def gradients(e_ref, k_ref, v_ref, g_ref, y_ref, block):
    first = pl.program_id(0) * (k_ref.shape[0] // block)
    part = y_ref.shape[1] - EXTRA
    each = block // part
    flip = mirror()
    for n, p, at, lanes in squares(k_ref, block):
        o = 2 * PARTS - 1 - p
        senders = range(n * each, (n + 1) * each)
        w = jnp.concatenate([y_ref[s, :part, lanes] for s in senders], axis=0).astype(jnp.float32)
        back = jnp.concatenate(
            [y_ref[s, :part, o * TILE : (o + 1) * TILE] for s in senders], axis=0
        )
        gz = jnp.dot(back, flip, preferred_element_type=jnp.float32)
        v_real = v_ref[at, lanes].astype(jnp.float32) * power(e_ref, 2, first + n, p)
        k_real = k_ref[at, lanes].astype(jnp.float32) * power(e_ref, 1, first + n, p)
        g = g_ref[at, lanes].astype(jnp.float32)
        yield p, at, lanes, (g * w, gz * v_real, gz * k_real)


def peak_kernel(e_ref, k_ref, v_ref, g_ref, y_ref, out_ref, peak_ref, *, block):
    @pl.when(pl.program_id(0) == 0)
    def _():
        peak_ref[...] = jnp.zeros(peak_ref.shape, jnp.float32)

    for p, at, lanes, products in gradients(e_ref, k_ref, v_ref, g_ref, y_ref, block):
        for i, product in enumerate(products):
            top = jnp.max(jnp.abs(product), axis=0, keepdims=True)
            spot = slice(p * 4 + i, p * 4 + i + 1)
            peak_ref[spot, :] = jnp.maximum(peak_ref[spot, :], top)

    @pl.when(pl.program_id(0) == pl.num_programs(0) - 1)
    def _():
        for n in range(out_ref.shape[0]):
            out_ref[n] = peak_ref[...]


def scale_kernel(e_ref, k_ref, v_ref, g_ref, y_ref, peaks_ref, oq_ref, ok_ref, ov_ref, lag_ref, top_ref, *, block):
    top = jnp.max(peaks_ref[...], axis=0)
    for p in range(PARTS):
        for i in range(3):
            best = jnp.max(top[p * 4 + i : p * 4 + i + 1, :], axis=1, keepdims=True)
            top_ref[p : p + 1, i : i + 1] = best
    top = jnp.max(top, axis=1, keepdims=True)
    part = y_ref.shape[1] - EXTRA
    share = lag_ref.shape[1]
    mine = lag_ref.shape[0] // y_ref.shape[0]
    for s in range(y_ref.shape[0]):
        terms = [
            y_ref[s, part:, t * TILE : t * TILE + share].astype(jnp.float32) for t in range(TERMS)
        ]
        lag_ref[s * mine : (s + 1) * mine, :] = (terms[0] + (terms[1] + terms[2]))[:mine, :]
    inverse = 1.0 / (top + EPS)
    for p, at, lanes, products in gradients(e_ref, k_ref, v_ref, g_ref, y_ref, block):
        for i, (product, ref) in enumerate(zip(products, (oq_ref, ok_ref, ov_ref))):
            ref[at, lanes] = (product * inverse[p * 4 + i : p * 4 + i + 1, :]).astype(jnp.bfloat16)


def shards(q_vals, k_vals, v_vals, grad_out, exponents, filter_taps):
    channels, rows = q_vals.shape
    groups, taps = filter_taps.shape
    block = channels // exponents.shape[1]
    width = channels // groups
    ctx = lax.axis_size("ctx")
    ch = lax.axis_size("ch")
    part = channels // ctx
    mine = groups // ctx
    span = taps + TILE
    tall = 2 * block
    steps = (channels // tall,)
    exponents = exponents.transpose(0, 2, 1)
    scalars = pl.BlockSpec(exponents.shape, lambda b: (0, 0, 0))
    tile = pl.BlockSpec((tall, rows), lambda b: (b, 0))
    double = pl.BlockSpec((tall, 2 * rows), lambda b: (b, 0))
    bf16 = jnp.bfloat16

    gated = pl.pallas_call(
        functools.partial(gate_kernel, block=block),
        grid=steps,
        in_specs=[scalars] + [tile] * 4,
        out_specs=double,
        out_shape=jax.ShapeDtypeStruct((channels, 2 * rows), bf16),
        name="gate",
    )(exponents, q_vals, k_vals, v_vals, grad_out)
    swapped = lax.all_to_all(gated, "ctx", split_axis=0, concat_axis=0, tiled=True)

    own_taps = lax.dynamic_slice_in_dim(filter_taps, lax.axis_index("ctx") * mine, mine, 0)
    count = ctx * PARTS
    lead = taps // TILE
    pair = pltpu.VMEM(((ctx + lead // 2) * width, 2 * TILE), bf16)
    scratch = [
        pltpu.VMEM((span + TILE, 2 * TILE), bf16),
        pair,
        pair,
        pltpu.VMEM((count * width, TILE), bf16),
        pltpu.VMEM(((count + lead) * width, TILE), bf16),
    ]
    resident = pl.BlockSpec(memory_space=pltpu.VMEM)
    y = pl.pallas_call(
        functools.partial(conv_kernel, width=width),
        in_specs=[resident, resident],
        out_specs=resident,
        out_shape=jax.ShapeDtypeStruct((ctx, part + EXTRA, 2 * rows), bf16),
        scratch_shapes=[pltpu.VMEM((ctx, EXTRA, taps // ctx), jnp.float32)] + scratch * mine,
        name="conv",
    )(own_taps, pltpu.with_memory_space_constraint(swapped.reshape(ctx, part, 2 * rows), pltpu.VMEM))

    y = lax.all_to_all(y, "ctx", split_axis=0, concat_axis=0, tiled=True)
    mixed = pl.BlockSpec((tall // part, part + EXTRA, 2 * rows), lambda b: (b, 0, 0))
    every = pl.BlockSpec((ch, 8, TILE), lambda b: (0, 0, 0))
    peaks = pl.pallas_call(
        functools.partial(peak_kernel, block=block),
        grid=steps,
        in_specs=[scalars] + [tile] * 3 + [mixed],
        out_specs=every,
        out_shape=jax.ShapeDtypeStruct((ch, 8, TILE), jnp.float32),
        scratch_shapes=[pltpu.VMEM((8, TILE), jnp.float32)],
        name="peak",
    )(exponents, k_vals, v_vals, grad_out, y)
    peaks = lax.all_to_all(peaks, "ch", split_axis=0, concat_axis=0, tiled=True)

    oq, ok, ov, grad_filter, top = pl.pallas_call(
        functools.partial(scale_kernel, block=block),
        grid=steps,
        in_specs=[scalars] + [tile] * 3 + [mixed, every],
        out_specs=[tile] * 3
        + [
            pl.BlockSpec((groups // steps[0], taps // ctx), lambda b: (b, 0)),
            pl.BlockSpec((PARTS, 3), lambda b: (0, 0)),
        ],
        out_shape=[jax.ShapeDtypeStruct((channels, rows), bf16)] * 3
        + [
            jax.ShapeDtypeStruct((groups, taps // ctx), jnp.float32),
            jax.ShapeDtypeStruct((PARTS, 3), jnp.float32),
        ],
        name="scale",
    )(exponents, k_vals, v_vals, grad_out, y, peaks)
    return oq, ok, ov, grad_filter, top.T


def solution(mesh):
    in_specs = (
        P("ch", "ctx"),
        P("ch", "ctx"),
        P("ch", "ctx"),
        P("ch", "ctx"),
        P(None, "ch", "ctx"),
        P("ch", None),
    )
    out_specs = (P("ch", "ctx"), P("ch", "ctx"), P("ch", "ctx"), P("ch", "ctx"), P(None, "ctx"))
    return jax.shard_map(shards, mesh=mesh, in_specs=in_specs, out_specs=out_specs, check_vma=False)
```

```python
import functools

import jax
import jax.numpy as jnp
from jax import lax
from jax.experimental import pallas as pl
from jax.experimental.pallas import tpu as pltpu
from jax.sharding import PartitionSpec as P

EPS = 1e-06
TILE = 128


def power(e_ref, i, b, p):
    exponent = e_ref[i]
    rows = lax.broadcasted_iota(jnp.int32, exponent.shape, 0)
    lanes = lax.broadcasted_iota(jnp.int32, exponent.shape, 1)
    value = lax.shift_left(jnp.ones_like(exponent), exponent + 8).astype(jnp.float32) * (2.0 ** -8)
    value = jnp.where((rows == p) & (lanes == b), value, 0.0)
    return jnp.sum(jnp.sum(value, axis=0, keepdims=True), axis=1, keepdims=True)


def mirror():
    shape = (TILE, TILE)
    rows = lax.broadcasted_iota(jnp.int32, shape, 0)
    lanes = lax.broadcasted_iota(jnp.int32, shape, 1)
    return (rows + lanes == TILE - 1).astype(jnp.float32).astype(jnp.bfloat16)


def mirrored(values, flip, terms):
    pieces = []
    rest = values
    for _ in range(terms):
        piece = rest.astype(jnp.bfloat16)
        pieces.append(piece)
        rest = rest - piece.astype(jnp.float32)
    return jnp.dot(
        jnp.concatenate(pieces, axis=1),
        jnp.concatenate([flip] * terms, axis=0),
        preferred_element_type=jnp.float32,
    )


def squares(ref, block):
    for n in range(ref.shape[0] // block):
        for p in range(PARTS):
            yield n, p, slice(n * block, (n + 1) * block), slice(p * TILE, (p + 1) * TILE)


PARTS = 2
TERMS = 3
EXTRA = 8


def gate_kernel(e_ref, q_ref, k_ref, v_ref, g_ref, out_ref, *, block):
    first = pl.program_id(0) * (q_ref.shape[0] // block)
    flip = mirror()
    for n, p, at, lanes in squares(q_ref, block):
        b = first + n
        q_real = q_ref[at, lanes].astype(jnp.float32) * power(e_ref, 0, b, p)
        k_real = k_ref[at, lanes].astype(jnp.float32) * power(e_ref, 1, b, p)
        v_real = v_ref[at, lanes].astype(jnp.float32) * power(e_ref, 2, b, p)
        out_ref[at, lanes] = (k_real * v_real).astype(jnp.bfloat16)
        gw = (q_real * g_ref[at, lanes].astype(jnp.float32)).astype(jnp.bfloat16)
        o = 2 * PARTS - 1 - p
        out_ref[at, o * TILE : (o + 1) * TILE] = jnp.dot(
            gw, flip, preferred_element_type=jnp.float32
        ).astype(jnp.bfloat16)


def conv_kernel(taps_ref, x_ref, y_ref, lag_ref, *scratch, width):
    blocks, part, lanes = x_ref.shape
    groups, taps = taps_ref.shape
    y_ref[:, part:, :] = jnp.zeros((blocks, y_ref.shape[1] - part, lanes), jnp.bfloat16)
    each = len(scratch) // groups
    for g in range(groups):
        one_group(g, taps_ref, x_ref, y_ref, lag_ref, *scratch[g * each : (g + 1) * each], width)
    rest = lag_ref[...]
    for term in range(TERMS):
        piece = rest.astype(jnp.bfloat16)
        y_ref[:, part : part + rest.shape[1], term * TILE : term * TILE + rest.shape[2]] = piece
        rest = rest - piece.astype(jnp.float32)


def one_group(g, taps_ref, x_ref, y_ref, lag_ref, toe_ref, z_ref, b_ref, own_ref, u_ref, width):
    blocks = x_ref.shape[0]
    taps = taps_ref.shape[1]
    span = taps + TILE
    tiles = span // TILE
    lead = tiles - 1
    count = blocks * PARTS
    own = slice(g * width, (g + 1) * width)

    row = taps_ref[g : g + 1, :].astype(jnp.bfloat16).astype(jnp.float32)
    row = jnp.concatenate([row, jnp.zeros((1, TILE), jnp.float32)], axis=1)
    row = jnp.broadcast_to(row, (8, span))
    low = pltpu.roll(row, 0, 1, stride=1, stride_axis=0)
    high = pltpu.roll(row, 8, 1, stride=1, stride_axis=0)
    base = jnp.concatenate([low, high], axis=0).astype(jnp.bfloat16)
    blank = jnp.zeros((TILE, TILE), jnp.bfloat16)
    toe_ref[0:TILE, 0:TILE] = blank
    toe_ref[tiles * TILE : (tiles + 1) * TILE, TILE : 2 * TILE] = blank
    for a in range(0, TILE, 16):
        rolled = pltpu.roll(base, a, 1) if a else base
        for d in range(tiles):
            piece = rolled[:, d * TILE : (d + 1) * TILE]
            toe_ref[(d + 1) * TILE + a : (d + 1) * TILE + a + 16, 0:TILE] = piece
            toe_ref[d * TILE + a : d * TILE + a + 16, TILE : 2 * TILE] = piece

    def z_tile(t):
        t = t % count
        return x_ref[t // PARTS, own, (t % PARTS) * TILE : (t % PARTS + 1) * TILE]

    def back_tile(t):
        t = t % count
        o = PARTS + t % PARTS
        return x_ref[blocks - 1 - t // PARTS, own, o * TILE : (o + 1) * TILE]

    half = lead // 2
    for m in range(blocks + half):
        rows = slice(m * width, (m + 1) * width)
        for p in range(2):
            lanes = slice((1 - p) * TILE, (2 - p) * TILE)
            z_ref[rows, lanes] = z_tile(2 * (m - half) + p)
            b_ref[rows, lanes] = back_tile(2 * (m - half) + p)
    for n in range(count):
        own_ref[n * width : (n + 1) * width, :] = back_tile(n)
    for n in range(count + lead):
        u_ref[n * width : (n + 1) * width, :] = z_tile(count - 1 - n)

    def window(ref):
        return jnp.concatenate(
            [ref[(half - f) * width : (half - f + blocks) * width, :] for f in range(half + 1)], axis=1
        )

    w = jnp.dot(window(z_ref), toe_ref[...], preferred_element_type=jnp.float32)
    for n in range(blocks):
        y_ref[n, own, 0 : 2 * TILE] = w[n * width : (n + 1) * width, :].astype(jnp.bfloat16)
    gz = jnp.dot(window(b_ref), toe_ref[...], preferred_element_type=jnp.float32)
    for n in range(blocks):
        y_ref[blocks - 1 - n, own, 2 * TILE : 4 * TILE] = gz[n * width : (n + 1) * width, :].astype(
            jnp.bfloat16
        )

    shifted = jnp.concatenate(
        [u_ref[(lead - d) * width : (lead - d + count) * width, :] for d in range(tiles)], axis=1
    )
    cross = lax.dot_general(
        own_ref[...], shifted, (((0,), (0,)), ((), ())), preferred_element_type=jnp.float32
    )
    total = None
    for a in range(0, TILE, 8):
        turned = pltpu.roll(
            cross[a : a + 8, :], (a + span - TILE) % span, 1, stride=1, stride_axis=0
        )
        total = turned if total is None else total + turned
    diag = jnp.sum(total, axis=0, keepdims=True)
    pieces = taps // TILE
    stacked = jnp.concatenate([diag[:, n * TILE : (n + 1) * TILE] for n in range(pieces)], axis=0)
    stacked = mirrored(stacked, mirror(), 3)
    share = lag_ref.shape[2]
    for r in range(blocks):
        n = pieces - 1 - r * share // TILE
        at = r * share % TILE
        lag_ref[r, g : g + 1, :] = stacked[n : n + 1, at : at + share]


def gradients(e_ref, k_ref, v_ref, g_ref, y_ref, block):
    part = y_ref.shape[1] - EXTRA
    each = block // part
    flip = mirror()
    for n, p, at, lanes in squares(k_ref, block):
        o = 2 * PARTS - 1 - p
        senders = range(n * each, (n + 1) * each)
        w = jnp.concatenate([y_ref[s, :part, lanes] for s in senders], axis=0).astype(jnp.float32)
        back = jnp.concatenate(
            [y_ref[s, :part, o * TILE : (o + 1) * TILE] for s in senders], axis=0
        )
        gz = jnp.dot(back, flip, preferred_element_type=jnp.float32)
        v_real = v_ref[at, lanes].astype(jnp.float32) * power(e_ref, 2, n, p)
        k_real = k_ref[at, lanes].astype(jnp.float32) * power(e_ref, 1, n, p)
        g = g_ref[at, lanes].astype(jnp.float32)
        yield p, at, lanes, (g * w, gz * v_real, gz * k_real)


def peak_kernel(e_ref, k_ref, v_ref, g_ref, y_ref, out_ref, *, block):
    tops = {}
    for p, at, lanes, products in gradients(e_ref, k_ref, v_ref, g_ref, y_ref, block):
        for i, product in enumerate(products):
            size = jnp.abs(product).reshape(block // 8, 8, TILE)
            top = jnp.max(size, axis=0)
            tops[p, i] = jnp.maximum(tops[p, i], top) if (p, i) in tops else top
    blank = jnp.zeros((1, TILE), jnp.float32)
    rows = []
    for p in range(PARTS):
        rows += [jnp.max(tops[p, i], axis=0, keepdims=True) for i in range(3)] + [blank]
    best = jnp.concatenate(rows, axis=0)
    out_ref[...] = best


def scale_kernel(e_ref, k_ref, v_ref, g_ref, y_ref, peaks_ref, other_ref, oq_ref, ok_ref, ov_ref, lag_ref, top_ref, *, block):
    top = jnp.maximum(peaks_ref[...], other_ref[...])
    for p in range(PARTS):
        for i in range(3):
            best = jnp.max(top[p * 4 + i : p * 4 + i + 1, :], axis=1, keepdims=True)
            top_ref[p : p + 1, i : i + 1] = best
    top = jnp.max(top, axis=1, keepdims=True)
    part = y_ref.shape[1] - EXTRA
    share = lag_ref.shape[1]
    mine = lag_ref.shape[0] // y_ref.shape[0]
    for s in range(y_ref.shape[0]):
        terms = [
            y_ref[s, part:, t * TILE : t * TILE + share].astype(jnp.float32) for t in range(TERMS)
        ]
        lag_ref[s * mine : (s + 1) * mine, :] = (terms[0] + (terms[1] + terms[2]))[:mine, :]
    inverse = 1.0 / (top + EPS)
    for p, at, lanes, products in gradients(e_ref, k_ref, v_ref, g_ref, y_ref, block):
        for i, (product, ref) in enumerate(zip(products, (oq_ref, ok_ref, ov_ref))):
            ref[at, lanes] = (product * inverse[p * 4 + i : p * 4 + i + 1, :]).astype(jnp.bfloat16)


def partners(devices):
    rounds = []
    size = 2
    while size <= devices:
        if size == 4:
            rounds.append([i - i % 4 + 3 - i % 4 for i in range(devices)])
        else:
            rounds.append([i ^ (size // 2) for i in range(devices)])
        size *= 2
    return rounds


def shards(q_vals, k_vals, v_vals, grad_out, exponents, filter_taps):
    channels, rows = q_vals.shape
    groups, taps = filter_taps.shape
    block = channels // exponents.shape[1]
    width = channels // groups
    ctx = lax.axis_size("ctx")
    ch = lax.axis_size("ch")
    part = channels // ctx
    mine = groups // ctx
    span = taps + TILE
    tall = 2 * block
    steps = (channels // tall,)
    exponents = exponents.transpose(0, 2, 1)
    scalars = pl.BlockSpec(exponents.shape, lambda b: (0, 0, 0))
    tile = pl.BlockSpec((tall, rows), lambda b: (b, 0))
    double = pl.BlockSpec((tall, 2 * rows), lambda b: (b, 0))
    bf16 = jnp.bfloat16

    gated = pl.pallas_call(
        functools.partial(gate_kernel, block=block),
        grid=steps,
        in_specs=[scalars] + [tile] * 4,
        out_specs=double,
        out_shape=jax.ShapeDtypeStruct((channels, 2 * rows), bf16),
        name="gate",
    )(exponents, q_vals, k_vals, v_vals, grad_out)
    swapped = lax.all_to_all(gated, "ctx", split_axis=0, concat_axis=0, tiled=True)

    own_taps = lax.dynamic_slice_in_dim(filter_taps, lax.axis_index("ctx") * mine, mine, 0)
    count = ctx * PARTS
    lead = taps // TILE
    pair = pltpu.VMEM(((ctx + lead // 2) * width, 2 * TILE), bf16)
    scratch = [
        pltpu.VMEM((span + TILE, 2 * TILE), bf16),
        pair,
        pair,
        pltpu.VMEM((count * width, TILE), bf16),
        pltpu.VMEM(((count + lead) * width, TILE), bf16),
    ]
    resident = pl.BlockSpec(memory_space=pltpu.VMEM)
    y = pl.pallas_call(
        functools.partial(conv_kernel, width=width),
        in_specs=[resident, resident],
        out_specs=resident,
        out_shape=jax.ShapeDtypeStruct((ctx, part + EXTRA, 2 * rows), bf16),
        scratch_shapes=[pltpu.VMEM((ctx, EXTRA, taps // ctx), jnp.float32)] + scratch * mine,
        name="conv",
    )(own_taps, pltpu.with_memory_space_constraint(swapped.reshape(ctx, part, 2 * rows), pltpu.VMEM))

    y = lax.all_to_all(y, "ctx", split_axis=0, concat_axis=0, tiled=True)
    near = lambda value: pltpu.with_memory_space_constraint(value, pltpu.VMEM)
    held = (exponents, near(k_vals), near(v_vals), near(grad_out), near(y))
    peaks = pl.pallas_call(
        functools.partial(peak_kernel, block=block),
        in_specs=[resident] * 5,
        out_specs=resident,
        out_shape=jax.ShapeDtypeStruct((8, TILE), jnp.float32),
        name="peak",
    )(*held)
    for partner in partners(ch)[:-1]:
        peaks = jnp.maximum(peaks, lax.ppermute(peaks, "ch", list(enumerate(partner))))
    others = lax.ppermute(peaks, "ch", list(enumerate(partners(ch)[-1])))

    oq, ok, ov, grad_filter, top = pl.pallas_call(
        functools.partial(scale_kernel, block=block),
        in_specs=[resident] * 7,
        out_specs=[resident] * 5,
        out_shape=[jax.ShapeDtypeStruct((channels, rows), bf16)] * 3
        + [
            jax.ShapeDtypeStruct((groups, taps // ctx), jnp.float32),
            jax.ShapeDtypeStruct((PARTS, 3), jnp.float32),
        ],
        name="scale",
    )(*held, near(peaks), near(others))
    return oq, ok, ov, grad_filter, top.T


def solution(mesh):
    in_specs = (
        P("ch", "ctx"),
        P("ch", "ctx"),
        P("ch", "ctx"),
        P("ch", "ctx"),
        P(None, "ch", "ctx"),
        P("ch", None),
    )
    out_specs = (P("ch", "ctx"), P("ch", "ctx"), P("ch", "ctx"), P("ch", "ctx"), P(None, "ctx"))
    return jax.shard_map(shards, mesh=mesh, in_specs=in_specs, out_specs=out_specs, check_vma=False)
```

```python
import functools

import jax
import jax.numpy as jnp
from jax import lax
from jax.experimental import pallas as pl
from jax.experimental.pallas import tpu as pltpu
from jax.sharding import PartitionSpec as P

EPS = 1e-06
TILE = 128


def power(e_ref, i, b, p):
    exponent = e_ref[i]
    rows = lax.broadcasted_iota(jnp.int32, exponent.shape, 0)
    lanes = lax.broadcasted_iota(jnp.int32, exponent.shape, 1)
    value = lax.shift_left(jnp.ones_like(exponent), exponent + 8).astype(jnp.float32) * (2.0 ** -8)
    value = jnp.where((rows == p) & (lanes == b), value, 0.0)
    return jnp.sum(jnp.sum(value, axis=0, keepdims=True), axis=1, keepdims=True)


def mirror():
    shape = (TILE, TILE)
    rows = lax.broadcasted_iota(jnp.int32, shape, 0)
    lanes = lax.broadcasted_iota(jnp.int32, shape, 1)
    return (rows + lanes == TILE - 1).astype(jnp.float32).astype(jnp.bfloat16)


def mirrored(values, flip, terms):
    pieces = []
    rest = values
    for _ in range(terms):
        piece = rest.astype(jnp.bfloat16)
        pieces.append(piece)
        rest = rest - piece.astype(jnp.float32)
    return jnp.dot(
        jnp.concatenate(pieces, axis=1),
        jnp.concatenate([flip] * terms, axis=0),
        preferred_element_type=jnp.float32,
    )


def squares(ref, block):
    for n in range(ref.shape[0] // block):
        for p in range(PARTS):
            yield n, p, slice(n * block, (n + 1) * block), slice(p * TILE, (p + 1) * TILE)


PARTS = 2
TERMS = 3
EXTRA = 8


def gate_kernel(e_ref, q_ref, k_ref, v_ref, g_ref, out_ref, *, block):
    first = pl.program_id(0) * (q_ref.shape[0] // block)
    flip = mirror()
    for n, p, at, lanes in squares(q_ref, block):
        b = first + n
        q_real = q_ref[at, lanes].astype(jnp.float32) * power(e_ref, 0, b, p)
        k_real = k_ref[at, lanes].astype(jnp.float32) * power(e_ref, 1, b, p)
        v_real = v_ref[at, lanes].astype(jnp.float32) * power(e_ref, 2, b, p)
        out_ref[at, lanes] = (k_real * v_real).astype(jnp.bfloat16)
        gw = (q_real * g_ref[at, lanes].astype(jnp.float32)).astype(jnp.bfloat16)
        o = 2 * PARTS - 1 - p
        out_ref[at, o * TILE : (o + 1) * TILE] = jnp.dot(
            gw, flip, preferred_element_type=jnp.float32
        ).astype(jnp.bfloat16)


def conv_kernel(taps_ref, x_ref, y_ref, lag_ref, *scratch, width):
    blocks, part, lanes = x_ref.shape
    groups, taps = taps_ref.shape
    y_ref[:, part:, :] = jnp.zeros((blocks, y_ref.shape[1] - part, lanes), jnp.bfloat16)
    each = len(scratch) // groups
    for g in range(groups):
        one_group(g, taps_ref, x_ref, y_ref, lag_ref, *scratch[g * each : (g + 1) * each], width)
    rest = lag_ref[...]
    for term in range(TERMS):
        piece = rest.astype(jnp.bfloat16)
        y_ref[:, part : part + rest.shape[1], term * TILE : term * TILE + rest.shape[2]] = piece
        rest = rest - piece.astype(jnp.float32)


def one_group(g, taps_ref, x_ref, y_ref, lag_ref, toe_ref, z_ref, b_ref, own_ref, u_ref, width):
    blocks = x_ref.shape[0]
    taps = taps_ref.shape[1]
    span = taps + TILE
    tiles = span // TILE
    lead = tiles - 1
    count = blocks * PARTS
    own = slice(g * width, (g + 1) * width)

    row = taps_ref[g : g + 1, :].astype(jnp.bfloat16).astype(jnp.float32)
    row = jnp.concatenate([row, jnp.zeros((1, TILE), jnp.float32)], axis=1)
    row = jnp.broadcast_to(row, (8, span))
    low = pltpu.roll(row, 0, 1, stride=1, stride_axis=0)
    high = pltpu.roll(row, 8, 1, stride=1, stride_axis=0)
    base = jnp.concatenate([low, high], axis=0).astype(jnp.bfloat16)
    blank = jnp.zeros((TILE, TILE), jnp.bfloat16)
    toe_ref[0:TILE, 0:TILE] = blank
    toe_ref[tiles * TILE : (tiles + 1) * TILE, TILE : 2 * TILE] = blank
    for a in range(0, TILE, 16):
        rolled = pltpu.roll(base, a, 1) if a else base
        for d in range(tiles):
            piece = rolled[:, d * TILE : (d + 1) * TILE]
            toe_ref[(d + 1) * TILE + a : (d + 1) * TILE + a + 16, 0:TILE] = piece
            toe_ref[d * TILE + a : d * TILE + a + 16, TILE : 2 * TILE] = piece

    def z_tile(t):
        t = t % count
        return x_ref[t // PARTS, own, (t % PARTS) * TILE : (t % PARTS + 1) * TILE]

    def back_tile(t):
        t = t % count
        o = PARTS + t % PARTS
        return x_ref[blocks - 1 - t // PARTS, own, o * TILE : (o + 1) * TILE]

    half = lead // 2
    for m in range(blocks + half):
        rows = slice(m * width, (m + 1) * width)
        for p in range(2):
            lanes = slice((1 - p) * TILE, (2 - p) * TILE)
            z_ref[rows, lanes] = z_tile(2 * (m - half) + p)
            b_ref[rows, lanes] = back_tile(2 * (m - half) + p)
    for n in range(count):
        own_ref[n * width : (n + 1) * width, :] = back_tile(n)
    for n in range(count + lead):
        u_ref[n * width : (n + 1) * width, :] = z_tile(count - 1 - n)

    def window(ref):
        return jnp.concatenate(
            [ref[(half - f) * width : (half - f + blocks) * width, :] for f in range(half + 1)], axis=1
        )

    w = jnp.dot(window(z_ref), toe_ref[...], preferred_element_type=jnp.float32)
    for n in range(blocks):
        y_ref[n, own, 0 : 2 * TILE] = w[n * width : (n + 1) * width, :].astype(jnp.bfloat16)
    gz = jnp.dot(window(b_ref), toe_ref[...], preferred_element_type=jnp.float32)
    for n in range(blocks):
        y_ref[blocks - 1 - n, own, 2 * TILE : 4 * TILE] = gz[n * width : (n + 1) * width, :].astype(
            jnp.bfloat16
        )

    shifted = jnp.concatenate(
        [u_ref[(lead - d) * width : (lead - d + count) * width, :] for d in range(tiles)], axis=1
    )
    cross = lax.dot_general(
        own_ref[...], shifted, (((0,), (0,)), ((), ())), preferred_element_type=jnp.float32
    )
    total = None
    for a in range(0, TILE, 8):
        turned = pltpu.roll(
            cross[a : a + 8, :], (a + span - TILE) % span, 1, stride=1, stride_axis=0
        )
        total = turned if total is None else total + turned
    diag = jnp.sum(total, axis=0, keepdims=True)
    pieces = taps // TILE
    stacked = jnp.concatenate([diag[:, n * TILE : (n + 1) * TILE] for n in range(pieces)], axis=0)
    stacked = mirrored(stacked, mirror(), 3)
    share = lag_ref.shape[2]
    for r in range(blocks):
        n = pieces - 1 - r * share // TILE
        at = r * share % TILE
        lag_ref[r, g : g + 1, :] = stacked[n : n + 1, at : at + share]


def gradients(e_ref, k_ref, v_ref, g_ref, y_ref, block):
    part = y_ref.shape[1] - EXTRA
    each = block // part
    flip = mirror()
    for n, p, at, lanes in squares(k_ref, block):
        o = 2 * PARTS - 1 - p
        senders = range(n * each, (n + 1) * each)
        w = jnp.concatenate([y_ref[s, :part, lanes] for s in senders], axis=0).astype(jnp.float32)
        back = jnp.concatenate(
            [y_ref[s, :part, o * TILE : (o + 1) * TILE] for s in senders], axis=0
        )
        gz = jnp.dot(back, flip, preferred_element_type=jnp.float32)
        v_real = v_ref[at, lanes].astype(jnp.float32) * power(e_ref, 2, n, p)
        k_real = k_ref[at, lanes].astype(jnp.float32) * power(e_ref, 1, n, p)
        g = g_ref[at, lanes].astype(jnp.float32)
        yield p, at, lanes, (g * w, gz * v_real, gz * k_real)


def peak_kernel(e_ref, k_ref, v_ref, g_ref, y_ref, out_ref, *, block):
    tops = {}
    for p, at, lanes, products in gradients(e_ref, k_ref, v_ref, g_ref, y_ref, block):
        for i, product in enumerate(products):
            size = jnp.abs(product).reshape(block // 8, 8, TILE)
            top = jnp.max(size, axis=0)
            tops[p, i] = jnp.maximum(tops[p, i], top) if (p, i) in tops else top
    blank = jnp.zeros((1, TILE), jnp.float32)
    rows = []
    for p in range(PARTS):
        rows += [jnp.max(tops[p, i], axis=0, keepdims=True) for i in range(3)] + [blank]
    best = jnp.concatenate(rows, axis=0)
    out_ref[...] = best


def scale_kernel(e_ref, k_ref, v_ref, g_ref, y_ref, peaks_ref, other_ref, oq_ref, ok_ref, ov_ref, lag_ref, top_ref, *, block):
    top = jnp.maximum(peaks_ref[...], other_ref[...])
    for p in range(PARTS):
        for i in range(3):
            best = jnp.max(top[p * 4 + i : p * 4 + i + 1, :], axis=1, keepdims=True)
            top_ref[p : p + 1, i : i + 1] = best
    top = jnp.max(top, axis=1, keepdims=True)
    part = y_ref.shape[1] - EXTRA
    share = lag_ref.shape[1]
    mine = lag_ref.shape[0] // y_ref.shape[0]
    for s in range(y_ref.shape[0]):
        terms = [
            y_ref[s, part:, t * TILE : t * TILE + share].astype(jnp.float32) for t in range(TERMS)
        ]
        lag_ref[s * mine : (s + 1) * mine, :] = (terms[0] + (terms[1] + terms[2]))[:mine, :]
    inverse = 1.0 / (top + EPS)
    for p, at, lanes, products in gradients(e_ref, k_ref, v_ref, g_ref, y_ref, block):
        for i, (product, ref) in enumerate(zip(products, (oq_ref, ok_ref, ov_ref))):
            ref[at, lanes] = (product * inverse[p * 4 + i : p * 4 + i + 1, :]).astype(jnp.bfloat16)


def partners(devices):
    rounds = []
    size = 2
    while size <= devices:
        if size == 4:
            rounds.append([i - i % 4 + 3 - i % 4 for i in range(devices)])
        else:
            rounds.append([i ^ (size // 2) for i in range(devices)])
        size *= 2
    return rounds


def shards(q_vals, k_vals, v_vals, grad_out, exponents, filter_taps):
    channels, rows = q_vals.shape
    groups, taps = filter_taps.shape
    block = channels // exponents.shape[1]
    width = channels // groups
    ctx = lax.axis_size("ctx")
    ch = lax.axis_size("ch")
    part = channels // ctx
    mine = groups // ctx
    span = taps + TILE
    tall = block
    steps = (channels // tall,)
    exponents = exponents.transpose(0, 2, 1)
    scalars = pl.BlockSpec(exponents.shape, lambda b: (0, 0, 0))
    tile = pl.BlockSpec((tall, rows), lambda b: (b, 0))
    double = pl.BlockSpec((tall, 2 * rows), lambda b: (b, 0))
    bf16 = jnp.bfloat16

    gated = pl.pallas_call(
        functools.partial(gate_kernel, block=block),
        grid=steps,
        in_specs=[scalars] + [tile] * 4,
        out_specs=double,
        out_shape=jax.ShapeDtypeStruct((channels, 2 * rows), bf16),
        name="gate",
    )(exponents, q_vals, k_vals, v_vals, grad_out)
    swapped = lax.all_to_all(gated, "ctx", split_axis=0, concat_axis=0, tiled=True)

    own_taps = lax.dynamic_slice_in_dim(filter_taps, lax.axis_index("ctx") * mine, mine, 0)
    count = ctx * PARTS
    lead = taps // TILE
    pair = pltpu.VMEM(((ctx + lead // 2) * width, 2 * TILE), bf16)
    scratch = [
        pltpu.VMEM((span + TILE, 2 * TILE), bf16),
        pair,
        pair,
        pltpu.VMEM((count * width, TILE), bf16),
        pltpu.VMEM(((count + lead) * width, TILE), bf16),
    ]
    resident = pl.BlockSpec(memory_space=pltpu.VMEM)
    y = pl.pallas_call(
        functools.partial(conv_kernel, width=width),
        in_specs=[resident, resident],
        out_specs=resident,
        out_shape=jax.ShapeDtypeStruct((ctx, part + EXTRA, 2 * rows), bf16),
        scratch_shapes=[pltpu.VMEM((ctx, EXTRA, taps // ctx), jnp.float32)] + scratch * mine,
        name="conv",
    )(own_taps, pltpu.with_memory_space_constraint(swapped.reshape(ctx, part, 2 * rows), pltpu.VMEM))

    y = lax.all_to_all(y, "ctx", split_axis=0, concat_axis=0, tiled=True)
    near = lambda value: pltpu.with_memory_space_constraint(value, pltpu.VMEM)
    held = (exponents, near(k_vals), near(v_vals), near(grad_out), near(y))
    peaks = pl.pallas_call(
        functools.partial(peak_kernel, block=block),
        in_specs=[resident] * 5,
        out_specs=resident,
        out_shape=pltpu.VMEM((8, TILE), jnp.float32),
        name="peak",
    )(*held)
    for partner in partners(ch)[:-1]:
        peaks = jnp.maximum(peaks, lax.ppermute(peaks, "ch", list(enumerate(partner))))
    others = lax.ppermute(peaks, "ch", list(enumerate(partners(ch)[-1])))

    oq, ok, ov, grad_filter, top = pl.pallas_call(
        functools.partial(scale_kernel, block=block),
        in_specs=[resident] * 7,
        out_specs=[resident] * 5,
        out_shape=[jax.ShapeDtypeStruct((channels, rows), bf16)] * 3
        + [
            jax.ShapeDtypeStruct((groups, taps // ctx), jnp.float32),
            jax.ShapeDtypeStruct((PARTS, 3), jnp.float32),
        ],
        name="scale",
    )(*held, near(peaks), near(others))
    return oq, ok, ov, grad_filter, top.T


def solution(mesh):
    in_specs = (
        P("ch", "ctx"),
        P("ch", "ctx"),
        P("ch", "ctx"),
        P("ch", "ctx"),
        P(None, "ch", "ctx"),
        P("ch", None),
    )
    out_specs = (P("ch", "ctx"), P("ch", "ctx"), P("ch", "ctx"), P("ch", "ctx"), P(None, "ctx"))
    return jax.shard_map(shards, mesh=mesh, in_specs=in_specs, out_specs=out_specs, check_vma=False)
```

```python
import functools

import jax
import jax.numpy as jnp
from jax import lax
from jax.experimental import pallas as pl
from jax.experimental.pallas import tpu as pltpu
from jax.sharding import PartitionSpec as P

EPS = 1e-06
TILE = 128


def power(e_ref, i, b, p):
    exponent = e_ref[i]
    rows = lax.broadcasted_iota(jnp.int32, exponent.shape, 0)
    lanes = lax.broadcasted_iota(jnp.int32, exponent.shape, 1)
    value = lax.shift_left(jnp.ones_like(exponent), exponent + 8).astype(jnp.float32) * (2.0 ** -8)
    value = jnp.where((rows == p) & (lanes == b), value, 0.0)
    return jnp.sum(jnp.sum(value, axis=0, keepdims=True), axis=1, keepdims=True)


def mirror():
    shape = (TILE, TILE)
    rows = lax.broadcasted_iota(jnp.int32, shape, 0)
    lanes = lax.broadcasted_iota(jnp.int32, shape, 1)
    return (rows + lanes == TILE - 1).astype(jnp.float32).astype(jnp.bfloat16)


def mirrored(values, flip, terms):
    pieces = []
    rest = values
    for _ in range(terms):
        piece = rest.astype(jnp.bfloat16)
        pieces.append(piece)
        rest = rest - piece.astype(jnp.float32)
    return jnp.dot(
        jnp.concatenate(pieces, axis=1),
        jnp.concatenate([flip] * terms, axis=0),
        preferred_element_type=jnp.float32,
    )


def squares(ref, block):
    for n in range(ref.shape[0] // block):
        for p in range(PARTS):
            yield n, p, slice(n * block, (n + 1) * block), slice(p * TILE, (p + 1) * TILE)


PARTS = 2
TERMS = 3
EXTRA = 8


def gate_kernel(e_ref, q_ref, k_ref, v_ref, g_ref, out_ref, *, block):
    first = pl.program_id(0) * (q_ref.shape[0] // block)
    flip = mirror()
    for n, p, at, lanes in squares(q_ref, block):
        b = first + n
        q_real = q_ref[at, lanes].astype(jnp.float32) * power(e_ref, 0, b, p)
        k_real = k_ref[at, lanes].astype(jnp.float32) * power(e_ref, 1, b, p)
        v_real = v_ref[at, lanes].astype(jnp.float32) * power(e_ref, 2, b, p)
        out_ref[at, lanes] = (k_real * v_real).astype(jnp.bfloat16)
        gw = (q_real * g_ref[at, lanes].astype(jnp.float32)).astype(jnp.bfloat16)
        o = 2 * PARTS - 1 - p
        out_ref[at, o * TILE : (o + 1) * TILE] = jnp.dot(
            gw, flip, preferred_element_type=jnp.float32
        ).astype(jnp.bfloat16)


def conv_kernel(taps_ref, x_ref, y_ref, lag_ref, *scratch, width):
    blocks, part, lanes = x_ref.shape
    groups, taps = taps_ref.shape
    y_ref[:, part:, :] = jnp.zeros((blocks, y_ref.shape[1] - part, lanes), jnp.bfloat16)
    each = len(scratch) // groups
    for g in range(groups):
        one_group(g, taps_ref, x_ref, y_ref, lag_ref, *scratch[g * each : (g + 1) * each], width)
    rest = lag_ref[...]
    for term in range(TERMS):
        piece = rest.astype(jnp.bfloat16)
        y_ref[:, part : part + rest.shape[1], term * TILE : term * TILE + rest.shape[2]] = piece
        rest = rest - piece.astype(jnp.float32)


def one_group(g, taps_ref, x_ref, y_ref, lag_ref, toe_ref, z_ref, b_ref, own_ref, u_ref, width):
    blocks = x_ref.shape[0]
    taps = taps_ref.shape[1]
    span = taps + TILE
    tiles = span // TILE
    lead = tiles - 1
    count = blocks * PARTS
    own = slice(g * width, (g + 1) * width)

    row = taps_ref[g : g + 1, :].astype(jnp.bfloat16).astype(jnp.float32)
    row = jnp.concatenate([row, jnp.zeros((1, TILE), jnp.float32)], axis=1)
    row = jnp.broadcast_to(row, (8, span))
    low = pltpu.roll(row, 0, 1, stride=1, stride_axis=0)
    high = pltpu.roll(row, 8, 1, stride=1, stride_axis=0)
    base = jnp.concatenate([low, high], axis=0).astype(jnp.bfloat16)
    blank = jnp.zeros((TILE, TILE), jnp.bfloat16)
    toe_ref[0:TILE, 0:TILE] = blank
    toe_ref[tiles * TILE : (tiles + 1) * TILE, TILE : 2 * TILE] = blank
    for a in range(0, TILE, 16):
        rolled = pltpu.roll(base, a, 1) if a else base
        for d in range(tiles):
            piece = rolled[:, d * TILE : (d + 1) * TILE]
            toe_ref[(d + 1) * TILE + a : (d + 1) * TILE + a + 16, 0:TILE] = piece
            toe_ref[d * TILE + a : d * TILE + a + 16, TILE : 2 * TILE] = piece

    def z_tile(t):
        t = t % count
        return x_ref[t // PARTS, own, (t % PARTS) * TILE : (t % PARTS + 1) * TILE]

    def back_tile(t):
        t = t % count
        o = PARTS + t % PARTS
        return x_ref[blocks - 1 - t // PARTS, own, o * TILE : (o + 1) * TILE]

    half = lead // 2
    for m in range(blocks + half):
        rows = slice(m * width, (m + 1) * width)
        for p in range(2):
            lanes = slice((1 - p) * TILE, (2 - p) * TILE)
            z_ref[rows, lanes] = z_tile(2 * (m - half) + p)
            b_ref[rows, lanes] = back_tile(2 * (m - half) + p)
    for n in range(count):
        own_ref[n * width : (n + 1) * width, :] = back_tile(n)
    for n in range(count + lead):
        u_ref[n * width : (n + 1) * width, :] = z_tile(count - 1 - n)

    def window(ref):
        return jnp.concatenate(
            [ref[(half - f) * width : (half - f + blocks) * width, :] for f in range(half + 1)], axis=1
        )

    w = jnp.dot(window(z_ref), toe_ref[...], preferred_element_type=jnp.float32)
    for n in range(blocks):
        y_ref[n, own, 0 : 2 * TILE] = w[n * width : (n + 1) * width, :].astype(jnp.bfloat16)
    gz = jnp.dot(window(b_ref), toe_ref[...], preferred_element_type=jnp.float32)
    for n in range(blocks):
        y_ref[blocks - 1 - n, own, 2 * TILE : 4 * TILE] = gz[n * width : (n + 1) * width, :].astype(
            jnp.bfloat16
        )

    shifted = jnp.concatenate(
        [u_ref[(lead - d) * width : (lead - d + count) * width, :] for d in range(tiles)], axis=1
    )
    cross = lax.dot_general(
        own_ref[...], shifted, (((0,), (0,)), ((), ())), preferred_element_type=jnp.float32
    )
    total = None
    for a in range(0, TILE, 8):
        turned = pltpu.roll(
            cross[a : a + 8, :], (a + span - TILE) % span, 1, stride=1, stride_axis=0
        )
        total = turned if total is None else total + turned
    diag = jnp.sum(total, axis=0, keepdims=True)
    pieces = taps // TILE
    stacked = jnp.concatenate([diag[:, n * TILE : (n + 1) * TILE] for n in range(pieces)], axis=0)
    stacked = mirrored(stacked, mirror(), 3)
    share = lag_ref.shape[2]
    for r in range(blocks):
        n = pieces - 1 - r * share // TILE
        at = r * share % TILE
        lag_ref[r, g : g + 1, :] = stacked[n : n + 1, at : at + share]


def gradients(e_ref, k_ref, v_ref, g_ref, y_ref, block):
    part = y_ref.shape[1] - EXTRA
    each = block // part
    flip = mirror()
    for n, p, at, lanes in squares(k_ref, block):
        o = 2 * PARTS - 1 - p
        senders = range(n * each, (n + 1) * each)
        w = jnp.concatenate([y_ref[s, :part, lanes] for s in senders], axis=0).astype(jnp.float32)
        back = jnp.concatenate(
            [y_ref[s, :part, o * TILE : (o + 1) * TILE] for s in senders], axis=0
        )
        gz = jnp.dot(back, flip, preferred_element_type=jnp.float32)
        v_real = v_ref[at, lanes].astype(jnp.float32) * power(e_ref, 2, n, p)
        k_real = k_ref[at, lanes].astype(jnp.float32) * power(e_ref, 1, n, p)
        g = g_ref[at, lanes].astype(jnp.float32)
        yield p, at, lanes, (g * w, gz * v_real, gz * k_real)


def peak_kernel(e_ref, k_ref, v_ref, g_ref, y_ref, out_ref, *, block):
    tops = {}
    for p, at, lanes, products in gradients(e_ref, k_ref, v_ref, g_ref, y_ref, block):
        for i, product in enumerate(products):
            size = jnp.abs(product).reshape(block // 8, 8, TILE)
            top = jnp.max(size, axis=0)
            tops[p, i] = jnp.maximum(tops[p, i], top) if (p, i) in tops else top
    blank = jnp.zeros((1, TILE), jnp.float32)
    rows = []
    for p in range(PARTS):
        rows += [jnp.max(tops[p, i], axis=0, keepdims=True) for i in range(3)] + [blank]
    best = jnp.concatenate(rows, axis=0)
    out_ref[...] = best


def scale_kernel(e_ref, k_ref, v_ref, g_ref, y_ref, peaks_ref, other_ref, oq_ref, ok_ref, ov_ref, lag_ref, top_ref, *, block):
    top = jnp.maximum(peaks_ref[...], other_ref[...])
    for p in range(PARTS):
        for i in range(3):
            best = jnp.max(top[p * 4 + i : p * 4 + i + 1, :], axis=1, keepdims=True)
            top_ref[p : p + 1, i : i + 1] = best
    top = jnp.max(top, axis=1, keepdims=True)
    part = y_ref.shape[1] - EXTRA
    share = lag_ref.shape[1]
    mine = lag_ref.shape[0] // y_ref.shape[0]
    for s in range(y_ref.shape[0]):
        terms = [
            y_ref[s, part:, t * TILE : t * TILE + share].astype(jnp.float32) for t in range(TERMS)
        ]
        lag_ref[s * mine : (s + 1) * mine, :] = (terms[0] + (terms[1] + terms[2]))[:mine, :]
    inverse = 1.0 / (top + EPS)
    for p, at, lanes, products in gradients(e_ref, k_ref, v_ref, g_ref, y_ref, block):
        for i, (product, ref) in enumerate(zip(products, (oq_ref, ok_ref, ov_ref))):
            ref[at, lanes] = (product * inverse[p * 4 + i : p * 4 + i + 1, :]).astype(jnp.bfloat16)


def partners(devices):
    rounds = []
    size = 2
    while size <= devices:
        if size == 4:
            rounds.append([i - i % 4 + 3 - i % 4 for i in range(devices)])
        else:
            rounds.append([i ^ (size // 2) for i in range(devices)])
        size *= 2
    return rounds


def shards(q_vals, k_vals, v_vals, grad_out, exponents, filter_taps):
    channels, rows = q_vals.shape
    groups, taps = filter_taps.shape
    block = channels // exponents.shape[1]
    width = channels // groups
    ctx = lax.axis_size("ctx")
    ch = lax.axis_size("ch")
    part = channels // ctx
    mine = groups // ctx
    span = taps + TILE
    tall = 4 * block
    steps = (channels // tall,)
    exponents = exponents.transpose(0, 2, 1)
    scalars = pl.BlockSpec(exponents.shape, lambda b: (0, 0, 0))
    tile = pl.BlockSpec((tall, rows), lambda b: (b, 0))
    double = pl.BlockSpec((tall, 2 * rows), lambda b: (b, 0))
    bf16 = jnp.bfloat16

    gated = pl.pallas_call(
        functools.partial(gate_kernel, block=block),
        grid=steps,
        in_specs=[scalars] + [tile] * 4,
        out_specs=double,
        out_shape=jax.ShapeDtypeStruct((channels, 2 * rows), bf16),
        name="gate",
    )(exponents, q_vals, k_vals, v_vals, grad_out)
    swapped = lax.all_to_all(gated, "ctx", split_axis=0, concat_axis=0, tiled=True)

    own_taps = lax.dynamic_slice_in_dim(filter_taps, lax.axis_index("ctx") * mine, mine, 0)
    count = ctx * PARTS
    lead = taps // TILE
    pair = pltpu.VMEM(((ctx + lead // 2) * width, 2 * TILE), bf16)
    scratch = [
        pltpu.VMEM((span + TILE, 2 * TILE), bf16),
        pair,
        pair,
        pltpu.VMEM((count * width, TILE), bf16),
        pltpu.VMEM(((count + lead) * width, TILE), bf16),
    ]
    resident = pl.BlockSpec(memory_space=pltpu.VMEM)
    y = pl.pallas_call(
        functools.partial(conv_kernel, width=width),
        in_specs=[resident, resident],
        out_specs=resident,
        out_shape=jax.ShapeDtypeStruct((ctx, part + EXTRA, 2 * rows), bf16),
        scratch_shapes=[pltpu.VMEM((ctx, EXTRA, taps // ctx), jnp.float32)] + scratch * mine,
        name="conv",
    )(own_taps, pltpu.with_memory_space_constraint(swapped.reshape(ctx, part, 2 * rows), pltpu.VMEM))

    y = lax.all_to_all(y, "ctx", split_axis=0, concat_axis=0, tiled=True)
    near = lambda value: pltpu.with_memory_space_constraint(value, pltpu.VMEM)
    held = (exponents, near(k_vals), near(v_vals), near(grad_out), near(y))
    peaks = pl.pallas_call(
        functools.partial(peak_kernel, block=block),
        in_specs=[resident] * 5,
        out_specs=resident,
        out_shape=pltpu.VMEM((8, TILE), jnp.float32),
        name="peak",
    )(*held)
    for partner in partners(ch)[:-1]:
        peaks = jnp.maximum(peaks, lax.ppermute(peaks, "ch", list(enumerate(partner))))
    others = lax.ppermute(peaks, "ch", list(enumerate(partners(ch)[-1])))

    oq, ok, ov, grad_filter, top = pl.pallas_call(
        functools.partial(scale_kernel, block=block),
        in_specs=[resident] * 7,
        out_specs=[resident] * 5,
        out_shape=[jax.ShapeDtypeStruct((channels, rows), bf16)] * 3
        + [
            jax.ShapeDtypeStruct((groups, taps // ctx), jnp.float32),
            jax.ShapeDtypeStruct((PARTS, 3), jnp.float32),
        ],
        name="scale",
    )(*held, near(peaks), near(others))
    return oq, ok, ov, grad_filter, top.T


def solution(mesh):
    in_specs = (
        P("ch", "ctx"),
        P("ch", "ctx"),
        P("ch", "ctx"),
        P("ch", "ctx"),
        P(None, "ch", "ctx"),
        P("ch", None),
    )
    out_specs = (P("ch", "ctx"), P("ch", "ctx"), P("ch", "ctx"), P("ch", "ctx"), P(None, "ctx"))
    return jax.shard_map(shards, mesh=mesh, in_specs=in_specs, out_specs=out_specs, check_vma=False)
```
